128 devices in a mesh: frame: 8 (over y, core), head: 8 (over x_hi, z), fsdp: 2 (over x_lo).
Axes of the slice: x: 4 (x_hi: 2, x_lo: 2; x = x_hi * 2 + x_lo), y: 4, z: 4, core: 2. Of those that a mesh axis runs over, the one named last changes fastest.
Arguments:
- queries: bfloat16 [2, 16, 256, 5120], P('fsdp', 'frame', 'head'), may hold values from -6 to 6
- key_rows: bfloat16 [2, 16, 256, 5120], P('fsdp', 'frame', 'head'), may hold values from -6 to 6
- value_rows: bfloat16 [2, 16, 256, 5120], P('fsdp', 'frame', 'head'), may hold values from -6 to 6
- saved_out: bfloat16 [2, 16, 256, 5120], P('fsdp', 'frame', 'head'), may hold values from -6 to 6
- cotangent: bfloat16 [2, 16, 256, 5120], P('fsdp', 'frame', 'head'), may hold values from -192 to 192
- out_weight: bfloat16 [5120, 5120], P('head'), may hold values from -0.078125 to 0.078125
- gate_table: float32 [64, 5120], replicated, may hold values from 0.25 to 2.5
- levels: int32 [16], P('frame'), may hold values from 0 to 63, as said below
- reach_flags: int32 [16, 2], replicated, may hold values from 0 to 1
Outputs:
- d_queries: bfloat16 [2, 16, 256, 5120], P('fsdp', 'frame', None, 'head')
- d_keys: bfloat16 [2, 16, 256, 5120], P('fsdp', 'frame', None, 'head')
- d_values: bfloat16 [2, 16, 256, 5120], P('fsdp', 'frame', None, 'head')
- d_weight: float32 [5120, 5120], P('head', ('frame', 'fsdp'))
The draws below stay inside these ranges and needn't reach their ends.
Inputs may be any that keep to these rules, and one draw needn't show every extreme that they name: `levels`: each frame's level is at least the level of the frame before it; the first frame has level 0 and the last frame level 63.
All inputs are finite; a program needn't handle non-finite values.
Results may differ from the reference program's by a relative error of at most 0.017.
Values may be sent and summed in bfloat16 or wider, within the bound.
A program may use at most 128 MiB of HBM per device.

```python
import math
from functools import reduce
import jax
import jax.numpy as jnp
from jax import lax

D = 5120
HD = 128
LEVELS = 64
FR_DEV = 2
TOKF = 256
FRAMES = 16
BATCH = 2


def draw_queries(key, part):
    own_key = jax.random.fold_in(key, 11)
    shape_all = (BATCH, FRAMES, TOKF, D)
    filled = jnp.clip(jax.random.normal(own_key, shape_all, jnp.float32), -6.0, 6.0)
    return filled.astype(jnp.bfloat16)


def draw_key_rows(key, part):
    own_key = jax.random.fold_in(key, 13)
    shape_all = (BATCH, FRAMES, TOKF, D)
    filled = jnp.clip(jax.random.normal(own_key, shape_all, jnp.float32), -6.0, 6.0)
    return filled.astype(jnp.bfloat16)


def draw_levels(key, part):
    increments = jax.random.randint(jax.random.fold_in(key, 23), (FRAMES,), 1, 5)
    increments = jnp.where(jnp.arange(FRAMES) == 0, 0, increments).astype(jnp.int32)
    running = jnp.cumsum(increments).astype(jnp.int32)
    return ((LEVELS - 1) * running // running[FRAMES - 1]).astype(jnp.int32)


def with_ends(result, stream_key, smallest, largest):
    longest = result.shape.index(max(result.shape))
    spots = []
    for shift in (0, 1):
        where = [jax.random.randint(jax.random.fold_in(stream_key, axis), (), 0, length) for axis, length in enumerate(result.shape)]
        where[longest] = (where[longest] + shift) % result.shape[longest]
        spots.append(tuple(where))
    return result.at[spots[0]].set(smallest).at[spots[1]].set(largest)


def raised(entries, stream_key, source, target, blocks, factor):
    owner, partner = [(jnp.arange(entries.shape[axis_at]) // (entries.shape[axis_at] // blocks)).reshape([-1 if axis == axis_at else 1 for axis in range(entries.ndim)]) for axis_at in (source, target)]
    chosen = jax.random.permutation(stream_key, blocks)[partner]
    strong = (owner == chosen) | (owner == (partner + blocks // 2) % blocks)
    return jnp.where(strong, factor * entries, entries)


def block_levels(rng, dims, cuts, smallest, largest):
    factor_of, own = 1.0, jax.random.fold_in(rng, 6)
    for axis_at, blocks in cuts:
        heights = jnp.exp(jax.random.uniform(jax.random.fold_in(own, axis_at), (blocks,), jnp.float32, smallest / len(cuts), largest / len(cuts)))
        factor_of = factor_of * jnp.repeat(heights, dims[axis_at] // blocks).reshape([-1 if axis == axis_at else 1 for axis in range(len(dims))])
    return factor_of


def bell_draw(stream_key, extent, deviation, reach, shards=(), held_as=jnp.bfloat16):
    values = jax.random.normal(stream_key, extent, jnp.float32) * deviation
    if len(shards) > 0:
        values = block_levels(stream_key, extent, shards, -0.22, 0.18) * values
    return jnp.clip(values, min=-reach, max=reach).astype(held_as)


def heavy_noise(key, dims, width, bound, cuts, heavy, held_as=jnp.bfloat16):
    result = width * jax.random.normal(key, dims, jnp.float32)
    if cuts:
        result = result * block_levels(key, dims, cuts, -0.22, 0.18)
    return jnp.clip(raised(result, jax.random.fold_in(key, 3), *heavy), -bound, bound).astype(held_as)


def setup_inputs(seed: int = 0) -> dict:
    key_of = jax.random.split(jax.random.key(seed), 10)
    return {
        "queries": draw_queries(jax.random.fold_in(key_of[9], 71), 0),
        "key_rows": draw_key_rows(jax.random.fold_in(key_of[9], 71), 0),
        "value_rows": bell_draw(key_of[2], (BATCH, FRAMES, TOKF, D), 1.0, 6.0, ((0, 2), (1, 8), (2, 8))),
        "saved_out": bell_draw(key_of[3], (BATCH, FRAMES, TOKF, D), 1.0, 6.0, ((0, 2), (1, 8), (2, 8))),
        "cotangent": heavy_noise(key_of[4], (BATCH, FRAMES, TOKF, D), 32.0, 192.0, ((0, 2), (1, 8), (2, 8)), (1, 3, 8, 2.0)),
        "out_weight": bell_draw(key_of[5], (D, D), D ** -0.5, 0.078125, ((0, 8),)),
        "gate_table": jnp.clip(jnp.exp(jax.random.uniform(key_of[6], (LEVELS, D), jnp.float32, math.log(0.25), math.log(2.5))), 0.25, 2.5),
        "levels": draw_levels(jax.random.fold_in(key_of[9], 71), 0),
        "reach_flags": with_ends(jax.random.randint(key_of[8], (FRAMES, 2), 0, 2), jax.random.fold_in(key_of[8], 1), 0, 1).astype(jnp.int32),
    }


NEG = -1e30


def block_scores(query_rows, key_block, inv_root):
    return jnp.einsum('thd,shd->hts', query_rows.astype(jnp.float32), key_block.astype(jnp.float32)) * inv_root


def row_stats(query_rows, key_list, allowed_set, inv_root):
    scores = [block_scores(query_rows, member, inv_root) for member in key_list]
    maxima = [jnp.max(jnp.where(allowed[None, None, :] > 0, score_block, NEG), axis=2) for score_block, allowed in zip(scores, allowed_set)]
    row_max = reduce(jnp.maximum, maxima)
    totals = [jnp.sum(jnp.where(allowed[None, None, :] > 0, jnp.exp(score_block - row_max[:, :, None]), 0.0), axis=2) for score_block, allowed in zip(scores, allowed_set)]
    return row_max + jnp.log(reduce(jnp.add, totals))


def block_grads(query_rows, d_out, key_block, value_block, log_total, row_delta, allowed, inv_root):
    scores = block_scores(query_rows, key_block, inv_root)
    prob_rows = jnp.where(allowed[None, None, :] > 0, jnp.exp(scores - log_total[:, :, None]), 0.0)
    probs_low = prob_rows.astype(jnp.bfloat16).astype(jnp.float32)
    d_wide = d_out.astype(jnp.float32)
    d_value = jnp.einsum('hts,thd->shd', probs_low, d_wide)
    d_probs = jnp.einsum('thd,shd->hts', d_wide, value_block.astype(jnp.float32))
    d_scores = (prob_rows * (d_probs - row_delta[:, :, None])).astype(jnp.bfloat16).astype(jnp.float32)
    d_query = jnp.einsum('hts,shd->thd', d_scores, key_block.astype(jnp.float32)) * inv_root
    d_key = jnp.einsum('hts,thd->shd', d_scores, query_rows.astype(jnp.float32)) * inv_root
    return d_query, d_key, d_value


def reach_mask(flag_value):
    half_count = TOKF // 2
    limit = half_count + (flag_value == 1).astype(jnp.int32) * (TOKF - half_count)
    return (jnp.arange(TOKF, dtype=jnp.int32) < limit).astype(jnp.float32)


def reference(queries, key_rows, value_rows, saved_out, cotangent, out_weight, gate_table, levels, reach_flags):
    inv_root = HD ** -0.5
    model_width = queries.shape[3]
    head_count = model_width // HD
    tokens_all = BATCH * FRAMES * TOKF
    choose = (levels[:, None] == jnp.arange(LEVELS, dtype=jnp.int32)[None, :]).astype(jnp.float32)
    frame_gain = jnp.dot(choose, gate_table, precision=lax.Precision.HIGHEST)
    gated = (cotangent.astype(jnp.float32) * frame_gain[None, :, None, :]).astype(jnp.bfloat16)
    d_low = jnp.einsum('bftd,ed->bfte', gated.astype(jnp.float32), out_weight.astype(jnp.float32)).astype(jnp.bfloat16)

    weight_grad = jnp.zeros((model_width, model_width), jnp.float32)
    for video in range(BATCH):
        for block_id in range(FRAMES // FR_DEV):
            first_frame = block_id * FR_DEV
            saved_rows = saved_out[video, first_frame:first_frame + FR_DEV].reshape(FR_DEV * TOKF, model_width)
            gated_rows = gated[video, first_frame:first_frame + FR_DEV].reshape(FR_DEV * TOKF, model_width)
            partial_sum = lax.dot_general(saved_rows, gated_rows, (((0,), (0,)), ((), ())), preferred_element_type=jnp.float32) / tokens_all
            rounded = lax.optimization_barrier(partial_sum.astype(jnp.bfloat16))
            weight_grad = weight_grad + rounded.astype(jnp.float32)

    def split_heads(array):
        return array.reshape(BATCH, FRAMES, TOKF, head_count, HD)

    q_five = split_heads(queries)
    k_five = split_heads(key_rows)
    v_five = split_heads(value_rows)
    o_five = split_heads(saved_out)
    d_five = split_heads(d_low)
    self_flag = jnp.ones((TOKF,), jnp.float32)
    video_q, video_k, video_v = [], [], []
    for video in range(BATCH):
        key_grads = [jnp.zeros((TOKF, head_count, HD), jnp.float32) for _ in range(FRAMES)]
        value_grads = [jnp.zeros((TOKF, head_count, HD), jnp.float32) for _ in range(FRAMES)]
        query_grads = []
        for frame_id in range(FRAMES):
            near_ids = []
            allowed_set = []
            for near_id in (frame_id - 1, frame_id, frame_id + 1):
                if 0 <= near_id < FRAMES:
                    near_ids.append(near_id)
                    if near_id == frame_id:
                        allowed_set.append(self_flag)
                    else:
                        column = 0 if near_id < frame_id else 1
                        allowed_set.append(reach_mask(reach_flags[frame_id, column]))
            query_rows = q_five[video, frame_id]
            log_total = row_stats(query_rows, [k_five[video, near_id] for near_id in near_ids], allowed_set, inv_root)
            row_delta = jnp.einsum('thd,thd->ht', d_five[video, frame_id].astype(jnp.float32), o_five[video, frame_id].astype(jnp.float32))
            query_grad = jnp.zeros((TOKF, head_count, HD), jnp.float32)
            for near_id, allowed in zip(near_ids, allowed_set):
                d_query, d_key, d_value = block_grads(query_rows, d_five[video, frame_id], k_five[video, near_id], v_five[video, near_id], log_total, row_delta, allowed, inv_root)
                query_grad = query_grad + d_query
                key_grads[near_id] = key_grads[near_id] + d_key
                value_grads[near_id] = value_grads[near_id] + d_value
            query_grads.append(query_grad)
        video_q.append(jnp.stack(query_grads))
        video_k.append(jnp.stack(key_grads))
        video_v.append(jnp.stack(value_grads))
    full_shape = (BATCH, FRAMES, TOKF, model_width)
    d_queries = jnp.stack(video_q).reshape(full_shape).astype(jnp.bfloat16)
    d_keys = jnp.stack(video_k).reshape(full_shape).astype(jnp.bfloat16)
    d_values = jnp.stack(video_v).reshape(full_shape).astype(jnp.bfloat16)
    return (d_queries, d_keys, d_values, weight_grad)
```

```python
import functools

import jax
import jax.numpy as jnp
from jax import lax
from jax.experimental import pallas as pl
from jax.experimental.pallas import tpu as pltpu
from jax.sharding import PartitionSpec as P

HD = 128
LEVELS = 64
TOKF = 256
NEG = -1e30
LOG2E = 1.4426950408889634
MESH = pl.DeviceIdType.MESH

NT = (((1,), (1,)), ((), ()))
NN = (((1,), (0,)), ((), ()))


def dot(a, b, dims):
    return lax.dot_general(a, b, dims, preferred_element_type=jnp.float32)


def kernel(
    tokens_all, flags,
    q_hbm, k_hbm, v_hbm, o_hbm, g_hbm, w_hbm,
    dq_hbm, dk_hbm, dv_hbm, dw_hbm,
    w_ref, g_ref, q_ref, o_ref, k_ref, v_ref, ot_ref, dacc, dlow, prob,
    s1_send, s1_recv, gsum, far_send, far_recv, near_send, near_recv, x_send, x_recv, dw_ref,
    own_k, own_v, h_send, h_recv, dq_ref, dk_ref, dv_ref,
    loc_sem, ex_send, ex_recv, ag_send, ag_recv, halo_ssem, halo_rsem,
    s1_ssem, s1_rsem, far_ssem, far_rsem, near_ssem, near_rsem, x_ssem, x_rsem, hg_ssem, hg_rsem, out_sem,
):
    f, h, s = lax.axis_index("frame"), lax.axis_index("head"), lax.axis_index("fsdp")
    nf = 8
    nh = 8
    y, c = f // 2, f % 2
    right, left = (f + 1) % nf, (f + 7) % nf
    up, down = (f + 2) % nf, (f + 6) % nf
    pair = 2 * y + 1 - c
    rows = 32
    wid = 640
    inv_root = HD ** (-0.5)

    def col(j):
        return pl.ds(pl.multiple_of(j * wid, 128), wid)

    my_rows = pl.ds(pl.multiple_of(h * rows, 32), rows)

    def chunk_of(t2):
        t = t2 // 2
        step = jnp.where(t == 0, 2, jnp.where(t == 1, 1, jnp.where(t == 2, 3, 0)))
        yt = (y + step) % 4
        return 2 * yt + jnp.where(t2 % 2 == 0, 1 - c, c)

    w_copy = pltpu.make_async_copy(w_hbm, w_ref, loc_sem.at[0])
    locals_ = [
        pltpu.make_async_copy(k_hbm.at[:, :, col(h)], k_ref.at[pl.ds(1, 2), my_rows, :], loc_sem.at[1]),
        pltpu.make_async_copy(v_hbm.at[:, :, col(h)], v_ref.at[pl.ds(1, 2), my_rows, :], loc_sem.at[2]),
        pltpu.make_async_copy(q_hbm.at[:, :, col(h)], q_ref.at[:, my_rows, :], loc_sem.at[3]),
        pltpu.make_async_copy(o_hbm.at[:, :, col(h)], o_ref.at[:, my_rows, :], loc_sem.at[4]),
        pltpu.make_async_copy(g_hbm, g_ref.at[:, my_rows, :], loc_sem.at[5]),
    ]

    barrier = pltpu.get_barrier_semaphore()
    for p in range(1, nh):
        pl.semaphore_signal(barrier, inc=1, device_id={"head": (h + p) % nh}, device_id_type=MESH)
    for other in (right, left, up, down):
        pl.semaphore_signal(barrier, inc=1, device_id={"frame": other}, device_id_type=MESH)
    pl.semaphore_signal(barrier, inc=1, device_id={"fsdp": 1 - s}, device_id_type=MESH)
    for copy in locals_:
        copy.start()
    w_copy.start()
    pl.semaphore_wait(barrier, nh - 1 + 5)

    def exchange(i, p):
        d = (h + p) % nh
        src, dst = [
            (k_hbm, k_ref.at[pl.ds(1, 2), my_rows, :]),
            (v_hbm, v_ref.at[pl.ds(1, 2), my_rows, :]),
            (q_hbm, q_ref.at[:, my_rows, :]),
            (o_hbm, o_ref.at[:, my_rows, :]),
        ][i]
        return pltpu.make_async_remote_copy(
            src_ref=src.at[:, :, col(d)], dst_ref=dst, send_sem=ex_send.at[i, p], recv_sem=ex_recv.at[i, p],
            device_id={"head": d}, device_id_type=MESH,
        )

    def gather(t2, p):
        d = (h + p) % nh
        cols = col(chunk_of(t2))
        return pltpu.make_async_remote_copy(
            src_ref=g_hbm.at[:, :, cols], dst_ref=g_ref.at[:, my_rows, cols],
            send_sem=ag_send.at[t2, p], recv_sem=ag_recv.at[t2, p],
            device_id={"head": d}, device_id_type=MESH,
        )

    order = (4, 2, 6, 1, 7, 3, 5)
    for i in range(4):
        for p in order:
            exchange(i, p).start()

    @pl.loop(0, 8)
    def _(t2):
        for p in order:
            gather(t2, p).start()

    def halo(i, which):
        ref = (k_ref, v_ref)[i]
        return pltpu.make_async_remote_copy(
            src_ref=ref.at[2 if which == 0 else 1], dst_ref=ref.at[0 if which == 0 else 3],
            send_sem=halo_ssem.at[i, which], recv_sem=halo_rsem.at[i, which],
            device_id={"frame": right if which == 0 else left}, device_id_type=MESH,
        )

    for i in range(2):
        locals_[i].wait()
        for p in range(1, nh):
            exchange(i, p).wait_recv()
        halo(i, 0).start()
        halo(i, 1).start()
    locals_[2].wait()
    for p in range(1, nh):
        exchange(2, p).wait_recv()
    halo(0, 0).wait_recv()
    halo(0, 1).wait_recv()

    def bias_of(fr, column, offset):
        target = fr + offset
        inside = (target >= 0) & (target < 2 * nf)
        chosen = flags[fr, column] == 1
        first = jnp.where(inside, 0.0, NEG).astype(jnp.float32)
        second = jnp.where(inside & chosen, 0.0, NEG).astype(jnp.float32)
        return first, second

    @pl.loop(0, 5)
    def _(hh):
        hs = pl.ds(pl.multiple_of(hh * HD, 128), HD)
        for lf in range(2):
            q = q_ref[lf, :, hs]
            parts = []
            for w in range(3):
                sc = dot(k_ref[lf + w, :, hs], q, NT) * (inv_root * LOG2E)
                if w == 1:
                    parts.append(sc)
                else:
                    first, second = bias_of(2 * f + lf, 0 if w == 0 else 1, w - 1)
                    parts.append(jnp.concatenate([sc[:128] + first, sc[128:] + second], axis=0))
            m = functools.reduce(jnp.maximum, [jnp.max(z, axis=0, keepdims=True) for z in parts])
            parts = [jnp.exp2(z - m) for z in parts]
            total = functools.reduce(jnp.add, [jnp.sum(z, axis=0, keepdims=True) for z in parts])
            inv = 1.0 / total
            for w in range(3):
                prob[2 * hh + lf, pl.ds(w * TOKF, TOKF), :] = parts[w] * inv

    locals_[3].wait()
    for p in range(1, nh):
        exchange(3, p).wait_recv()
    for lf in range(2):
        ot_ref[:, pl.ds(lf * TOKF, TOKF)] = o_ref[lf].astype(jnp.float32).T.astype(jnp.bfloat16)
    locals_[4].wait()
    w_copy.wait()
    dacc[...] = jnp.zeros_like(dacc)

    def s1(t):
        return pltpu.make_async_remote_copy(
            src_ref=s1_send.at[t], dst_ref=s1_recv.at[t], send_sem=s1_ssem.at[t], recv_sem=s1_rsem.at[t],
            device_id={"frame": pair}, device_id_type=MESH,
        )

    def far(i):
        return pltpu.make_async_remote_copy(
            src_ref=far_send.at[i], dst_ref=far_recv.at[i], send_sem=far_ssem.at[i], recv_sem=far_rsem.at[i],
            device_id={"frame": up if i == 0 else down}, device_id_type=MESH,
        )

    def near(i):
        return pltpu.make_async_remote_copy(
            src_ref=near_send.at[i], dst_ref=near_recv.at[i], send_sem=near_ssem.at[i], recv_sem=near_rsem.at[i],
            device_id={"frame": up if i == 0 else down}, device_id_type=MESH,
        )

    def one_chunk(t2):
        for p in range(1, nh):
            gather(t2, p).wait_recv()
        cols = col(chunk_of(t2))
        rhs = g_ref[:, :, cols].reshape(2 * TOKF, wid)
        dacc[...] += dot(rhs, w_ref[:, cols], NT)
        return dot(ot_ref[...], rhs, NN) * (1.0 / tokens_all)

    def finish_near(i):
        far(i).wait_recv()
        half = pl.ds(320 * i, 320)
        rest = pl.ds(320 * (1 - i), 320)
        near_send[i, half, :] = (gsum[1 + i, half, :] + far_recv[i].astype(jnp.float32)).astype(jnp.bfloat16)
        near_send[i, rest, :] = gsum[1 + i, rest, :].astype(jnp.bfloat16)
        near(i).start()

    @pl.loop(0, 4)
    def _(t):
        s1_send[t] = one_chunk(2 * t).astype(jnp.bfloat16)
        s1(t).start()

        @pl.when(t == 2)
        def _():
            finish_near(0)

        @pl.when(t == 3)
        def _():
            finish_near(1)

        gsum[t] = one_chunk(2 * t + 1)
        s1(t).wait_recv()
        gsum[t] += s1_recv[t].astype(jnp.float32)

        @pl.when(t == 0)
        def _():
            for i in range(2):
                far_send[i] = gsum[0, pl.ds(320 * i, 320), :].astype(jnp.bfloat16)
                far(i).start()

    for lf in range(2):
        dlow[lf] = dacc[pl.ds(lf * TOKF, TOKF), :].astype(jnp.bfloat16)
    halo(1, 0).wait_recv()
    halo(1, 1).wait_recv()

    x_copy = pltpu.make_async_remote_copy(
        src_ref=x_send, dst_ref=x_recv, send_sem=x_ssem, recv_sem=x_rsem,
        device_id={"fsdp": 1 - s}, device_id_type=MESH,
    )

    def halo_grad(i, hh):
        return pltpu.make_async_remote_copy(
            src_ref=h_send.at[i, hh], dst_ref=h_recv.at[i, hh], send_sem=hg_ssem.at[i, hh], recv_sem=hg_rsem.at[i, hh],
            device_id={"frame": left if i == 0 else right}, device_id_type=MESH,
        )

    @pl.loop(0, 5)
    def _(hh):
        hs = pl.ds(pl.multiple_of(hh * HD, 128), HD)
        gk = []
        gv = []
        for lf in range(2):
            q = q_ref[lf, :, hs]
            d_out = dlow[lf, :, hs]
            delta = jnp.sum(
                (d_out.astype(jnp.float32) * o_ref[lf, :, hs].astype(jnp.float32)).T, axis=0, keepdims=True
            )
            dq_t = jnp.zeros((HD, TOKF), jnp.float32)
            for w in range(3):
                pr = prob[2 * hh + lf, pl.ds(w * TOKF, TOKF), :]
                dp = dot(v_ref[lf + w, :, hs], d_out, NT)
                ds = (pr * (dp - delta)).astype(jnp.bfloat16)
                gv.append(dot(pr.astype(jnp.bfloat16), d_out, NN))
                gk.append(dot(ds, q, NN) * inv_root)
                kt = k_ref[lf + w, :, hs].astype(jnp.float32).T.astype(jnp.bfloat16)
                dq_t = dq_t + dot(kt, ds, NN)
            dq_ref[lf, :, hs] = (dq_t.T * inv_root).astype(jnp.bfloat16)
        h_send[0, hh, 0] = gk[0].astype(jnp.bfloat16)
        h_send[0, hh, 1] = gv[0].astype(jnp.bfloat16)
        h_send[1, hh, 0] = gk[5].astype(jnp.bfloat16)
        h_send[1, hh, 1] = gv[5].astype(jnp.bfloat16)
        halo_grad(0, hh).start()
        halo_grad(1, hh).start()
        own_k[0, :, hs] = gk[1] + gk[3]
        own_k[1, :, hs] = gk[2] + gk[4]
        own_v[0, :, hs] = gv[1] + gv[3]
        own_v[1, :, hs] = gv[2] + gv[4]

    dq_out = pltpu.make_async_copy(dq_ref, dq_hbm, out_sem.at[0])
    dq_out.start()

    near(0).wait_recv()
    near(1).wait_recv()
    gsum[3] += near_recv[0].astype(jnp.float32) + near_recv[1].astype(jnp.float32)
    x_send[...] = gsum[3, :, pl.ds(pl.multiple_of(256 * (1 - s), 128), 384)].astype(jnp.bfloat16)
    x_copy.start()

    @pl.loop(0, 5)
    def _(hh):
        hs = pl.ds(pl.multiple_of(hh * HD, 128), HD)
        halo_grad(0, hh).wait_recv()
        halo_grad(1, hh).wait_recv()
        dk_ref[0, :, hs] = (own_k[0, :, hs] + h_recv[1, hh, 0].astype(jnp.float32)).astype(jnp.bfloat16)
        dk_ref[1, :, hs] = (own_k[1, :, hs] + h_recv[0, hh, 0].astype(jnp.float32)).astype(jnp.bfloat16)
        dv_ref[0, :, hs] = (own_v[0, :, hs] + h_recv[1, hh, 1].astype(jnp.float32)).astype(jnp.bfloat16)
        dv_ref[1, :, hs] = (own_v[1, :, hs] + h_recv[0, hh, 1].astype(jnp.float32)).astype(jnp.bfloat16)

    dk_out = pltpu.make_async_copy(dk_ref, dk_hbm, out_sem.at[1])
    dv_out = pltpu.make_async_copy(dv_ref, dv_hbm, out_sem.at[2])
    dk_out.start()
    dv_out.start()

    x_copy.wait_recv()
    final = gsum[3, :, pl.ds(pl.multiple_of(256 * s, 128), 384)] + x_recv[...].astype(jnp.float32)
    dw_ref[...] = jnp.where(s == 0, final[:, :320], final[:, 64:384])
    dw_out = pltpu.make_async_copy(dw_ref, dw_hbm, out_sem.at[3])
    dw_out.start()

    for i in range(4):
        for p in range(1, nh):
            exchange(i, p).wait_send()

    @pl.loop(0, 8)
    def _(t2):
        for p in range(1, nh):
            gather(t2, p).wait_send()

    for i in range(2):
        for which in range(2):
            halo(i, which).wait_send()
        far(i).wait_send()
        near(i).wait_send()

    @pl.loop(0, 4)
    def _(t):
        s1(t).wait_send()

    @pl.loop(0, 5)
    def _(hh):
        halo_grad(0, hh).wait_send()
        halo_grad(1, hh).wait_send()

    x_copy.wait_send()
    for copy in (dq_out, dk_out, dv_out, dw_out):
        copy.wait()


def per_device(
    queries, key_rows, value_rows, saved_out, cotangent, out_weight, gate_table, levels, reach_flags
):
    frame_dev = queries.shape[1]
    tokens_all = lax.axis_size("fsdp") * frame_dev * lax.axis_size("frame") * TOKF
    choose = (levels[:, None] == jnp.arange(LEVELS, dtype=jnp.int32)[None, :]).astype(jnp.float32)
    frame_gain = jnp.dot(choose, gate_table, precision=lax.Precision.HIGHEST)
    gated = (cotangent.astype(jnp.float32) * frame_gain[None, :, None, :]).astype(jnp.bfloat16)

    bf, f32 = jnp.bfloat16, jnp.float32
    vm = pltpu.VMEM
    dma = pltpu.SemaphoreType.DMA
    hbm = pl.BlockSpec(memory_space=pl.ANY)
    out = jax.ShapeDtypeStruct((2, TOKF, 640), bf)
    dq, dk, dv, dw = pl.pallas_call(
        functools.partial(kernel, tokens_all),
        out_shape=(out, out, out, jax.ShapeDtypeStruct((640, 320), f32)),
        in_specs=[pl.BlockSpec(memory_space=pltpu.SMEM)] + [hbm] * 6,
        out_specs=(hbm,) * 4,
        scratch_shapes=[
            vm((640, 5120), bf),
            vm((2, TOKF, 5120), bf),
            vm((2, TOKF, 640), bf),
            vm((2, TOKF, 640), bf),
            vm((4, TOKF, 640), bf),
            vm((4, TOKF, 640), bf),
            vm((640, 2 * TOKF), bf),
            vm((2 * TOKF, 640), f32),
            vm((2, TOKF, 640), bf),
            vm((10, 3 * TOKF, TOKF), f32),
            vm((4, 640, 640), bf),
            vm((4, 640, 640), bf),
            vm((4, 640, 640), f32),
            vm((2, 320, 640), bf),
            vm((2, 320, 640), bf),
            vm((2, 640, 640), bf),
            vm((2, 640, 640), bf),
            vm((640, 384), bf),
            vm((640, 384), bf),
            vm((640, 320), f32),
            vm((2, TOKF, 640), f32),
            vm((2, TOKF, 640), f32),
            vm((2, 5, 2, TOKF, HD), bf),
            vm((2, 5, 2, TOKF, HD), bf),
            vm((2, TOKF, 640), bf),
            vm((2, TOKF, 640), bf),
            vm((2, TOKF, 640), bf),
            dma((6,)),
            dma((4, 8)), dma((4, 8)),
            dma((8, 8)), dma((8, 8)),
            dma((2, 2)), dma((2, 2)),
            dma((4,)), dma((4,)),
            dma((2,)), dma((2,)),
            dma((2,)), dma((2,)),
            dma(()), dma(()),
            dma((2, 5)), dma((2, 5)),
            dma((4,)),
        ],
        compiler_params=pltpu.CompilerParams(
            collective_id=0, has_side_effects=True, vmem_limit_bytes=67043328
        ),
        name="window_backward",
    )(
        reach_flags, queries[0], key_rows[0], value_rows[0], saved_out[0], gated[0], out_weight
    )
    return (dq[None], dk[None], dv[None], dw)


def solution(mesh):
    in_specs = (
        P("fsdp", "frame", "head", None),
        P("fsdp", "frame", "head", None),
        P("fsdp", "frame", "head", None),
        P("fsdp", "frame", "head", None),
        P("fsdp", "frame", "head", None),
        P("head", None),
        P(),
        P("frame"),
        P(),
    )
    out_specs = (
        P("fsdp", "frame", None, "head"),
        P("fsdp", "frame", None, "head"),
        P("fsdp", "frame", None, "head"),
        P("head", ("frame", "fsdp")),
    )
    return jax.shard_map(
        per_device, mesh=mesh, in_specs=in_specs, out_specs=out_specs, check_vma=False
    )
```

```python
import functools

import jax
import jax.numpy as jnp
from jax import lax
from jax.experimental import pallas as pl
from jax.experimental.pallas import tpu as pltpu
from jax.sharding import PartitionSpec as P

HD = 128
LEVELS = 64
TOKF = 256
NEG = -1e30
LOG2E = 1.4426950408889634
MESH = pl.DeviceIdType.MESH

NT = (((1,), (1,)), ((), ()))
NN = (((1,), (0,)), ((), ()))


def dot(a, b, dims):
    return lax.dot_general(a, b, dims, preferred_element_type=jnp.float32)


def kernel(
    tokens_all, flags, levels,
    q_hbm, k_hbm, v_hbm, o_hbm, c_hbm, w_hbm, gate_hbm,
    dq_hbm, dk_hbm, dv_hbm, dw_hbm,
    w_ref, g_ref, q_ref, o_ref, k_ref, v_ref, c_ref, gate_ref, ot_ref, dacc,
    s1_send, s1_recv, gsum, far_send, far_recv, near_send, near_recv, x_send, x_recv, dw_ref,
    own_k, own_v, h_send, h_recv, dq_ref, dk_ref, dv_ref,
    loc_sem, exo_send, exo_recv, ex_send, ex_recv, ag_send, ag_recv, halo_ssem, halo_rsem,
    s1_ssem, s1_rsem, far_ssem, far_rsem, near_ssem, near_rsem, x_ssem, x_rsem, hg_ssem, hg_rsem, out_sem, dw_sem,
):
    f, h, s = lax.axis_index("frame"), lax.axis_index("head"), lax.axis_index("fsdp")
    nf = 8
    nh = 8
    y, c = f // 2, f % 2
    xh, z = h // 4, h % 4
    zp, zm = (z + 1) % 4, (z + 3) % 4
    right, left = (f + 1) % nf, (f + 7) % nf
    up, down = (f + 2) % nf, (f + 6) % nf
    pair = 2 * y + 1 - c
    rows = 32
    wid = 640
    heads = 5
    inv_root = HD ** (-0.5)

    def col(j):
        return pl.ds(pl.multiple_of(j * wid, 128), wid)

    def rows_of(n):
        return pl.ds(pl.multiple_of(n * rows, 32), rows)

    my_rows = rows_of(h)

    def chunk_of(t2):
        t = t2 // 2
        step = jnp.where(t == 0, 2, jnp.where(t == 1, 1, jnp.where(t == 2, 3, 0)))
        yt = (y + step) % 4
        return 2 * yt + jnp.where(t2 % 2 == 0, 1 - c, c)

    def head_cols(d, hh):
        return pl.ds(pl.multiple_of(d * wid + hh * HD, 128), HD)

    c_copy = pltpu.make_async_copy(c_hbm, c_ref, loc_sem.at[0])
    gate_copy = pltpu.make_async_copy(gate_hbm, gate_ref, loc_sem.at[1])
    o_copy = pltpu.make_async_copy(o_hbm.at[:, :, col(h)], o_ref.at[:, my_rows, :], loc_sem.at[2])
    w_copy = pltpu.make_async_copy(w_hbm, w_ref, loc_sem.at[3])

    def own_copy(i, hh):
        src, dst = (
            (k_hbm, k_ref.at[hh, pl.ds(1, 2), my_rows, :]),
            (v_hbm, v_ref.at[hh, pl.ds(1, 2), my_rows, :]),
            (q_hbm, q_ref.at[hh, :, my_rows, :]),
        )[i]
        return pltpu.make_async_copy(src.at[:, :, head_cols(h, hh)], dst, ex_recv.at[hh, i, 0])

    barrier = pltpu.get_barrier_semaphore()
    for p in range(1, nh):
        pl.semaphore_signal(barrier, inc=1, device_id={"head": (h + p) % nh}, device_id_type=MESH)
    for other in (right, left, up, down):
        pl.semaphore_signal(barrier, inc=1, device_id={"frame": other}, device_id_type=MESH)
    pl.semaphore_signal(barrier, inc=1, device_id={"fsdp": 1 - s}, device_id_type=MESH)
    c_copy.start()
    gate_copy.start()
    o_copy.start()
    w_copy.start()

    @pl.loop(0, heads)
    def _(hh):
        for i in range(3):
            own_copy(i, hh).start()

    c_copy.wait()
    gate_copy.wait()
    for lf in range(2):
        gain = gate_ref[pl.ds(levels[lf], 1), :]
        g_ref[lf, my_rows, :] = (c_ref[lf].astype(jnp.float32) * gain).astype(jnp.bfloat16)
    pl.semaphore_wait(barrier, nh - 1 + 5)

    def o_exchange(p):
        d = (h + p) % nh
        return pltpu.make_async_remote_copy(
            src_ref=o_hbm.at[:, :, col(d)], dst_ref=o_ref.at[:, my_rows, :],
            send_sem=exo_send.at[p], recv_sem=exo_recv.at[p],
            device_id={"head": d}, device_id_type=MESH,
        )

    def exchange(i, hh, p):
        d = (h + p) % nh
        src, dst = (
            (k_hbm, k_ref.at[hh, pl.ds(1, 2), my_rows, :]),
            (v_hbm, v_ref.at[hh, pl.ds(1, 2), my_rows, :]),
            (q_hbm, q_ref.at[hh, :, my_rows, :]),
        )[i]
        return pltpu.make_async_remote_copy(
            src_ref=src.at[:, :, head_cols(d, hh)], dst_ref=dst,
            send_sem=ex_send.at[hh, i, p], recv_sem=ex_recv.at[hh, i, p],
            device_id={"head": d}, device_id_type=MESH,
        )

    def part(t2, n, half, idx, xt, zt):
        cols = col(chunk_of(t2))
        ref = g_ref.at[:, rows_of(n), cols] if half is None else g_ref.at[half, rows_of(n), cols]
        return pltpu.make_async_remote_copy(
            src_ref=ref, dst_ref=ref, send_sem=ag_send.at[t2, idx], recv_sem=ag_recv.at[t2, idx],
            device_id={"head": xt * 4 + zt}, device_id_type=MESH,
        )

    def gather(t2, idx):
        xo = 1 - xh
        return (
            lambda: part(t2, h, None, 0, xh, zp),
            lambda: part(t2, h, None, 1, xh, zm),
            lambda: part(t2, xh * 4 + zm, None, 2, xo, z),
            lambda: part(t2, xh * 4 + zp, None, 3, xo, z),
            lambda: part(t2, xh * 4 + zm, 0, 4, xh, zp),
            lambda: part(t2, xh * 4 + zp, 1, 5, xh, zm),
            lambda: part(t2, xo * 4 + zm, 0, 6, xh, zp),
            lambda: part(t2, xo * 4 + zm, 0, 7, xh, zm),
            lambda: part(t2, xo * 4 + zp, 1, 8, xh, zp),
            lambda: part(t2, xo * 4 + zp, 1, 9, xh, zm),
        )[idx]()

    def stage1(t2):
        gather(t2, 0).start()
        gather(t2, 1).start()

    def stage2(t2):
        gather(t2, 0).wait_recv()
        gather(t2, 2).start()
        gather(t2, 4).start()
        gather(t2, 1).wait_recv()
        gather(t2, 3).start()
        gather(t2, 5).start()

    def stage3(t2):
        gather(t2, 2).wait_recv()
        gather(t2, 6).start()
        gather(t2, 7).start()
        gather(t2, 3).wait_recv()
        gather(t2, 8).start()
        gather(t2, 9).start()

    order = (4, 2, 6, 1, 7, 3, 5)
    stage1(0)
    stage1(1)
    for p in order:
        o_exchange(p).start()

    def halo(i, hh, which):
        ref = (k_ref, v_ref)[i]
        return pltpu.make_async_remote_copy(
            src_ref=ref.at[hh, 2 if which == 0 else 1], dst_ref=ref.at[hh, 0 if which == 0 else 3],
            send_sem=halo_ssem.at[i, hh, which], recv_sem=halo_rsem.at[i, hh, which],
            device_id={"frame": right if which == 0 else left}, device_id_type=MESH,
        )

    def s1(t):
        return pltpu.make_async_remote_copy(
            src_ref=s1_send.at[t], dst_ref=s1_recv.at[t], send_sem=s1_ssem.at[t], recv_sem=s1_rsem.at[t],
            device_id={"frame": pair}, device_id_type=MESH,
        )

    def far(i):
        return pltpu.make_async_remote_copy(
            src_ref=far_send.at[i], dst_ref=far_recv.at[i], send_sem=far_ssem.at[i], recv_sem=far_rsem.at[i],
            device_id={"frame": up if i == 0 else down}, device_id_type=MESH,
        )

    def near(i):
        return pltpu.make_async_remote_copy(
            src_ref=near_send.at[i], dst_ref=near_recv.at[i], send_sem=near_ssem.at[i], recv_sem=near_rsem.at[i],
            device_id={"frame": up if i == 0 else down}, device_id_type=MESH,
        )

    def one_chunk(t2):
        for idx in range(4, 10):
            gather(t2, idx).wait_recv()
        cols = col(chunk_of(t2))
        rhs = g_ref[:, :, cols].reshape(2 * TOKF, wid)
        dacc[...] += dot(rhs, w_ref[:, cols], NT)
        return dot(ot_ref[...], rhs, NN) * (1.0 / tokens_all)

    def finish_near(i):
        far(i).wait_recv()
        half = pl.ds(320 * i, 320)
        rest = pl.ds(320 * (1 - i), 320)
        near_send[i, half, :] = (gsum[1 + i, half, :] + far_recv[i].astype(jnp.float32)).astype(jnp.bfloat16)
        near_send[i, rest, :] = gsum[1 + i, rest, :].astype(jnp.bfloat16)
        near(i).start()

    @pl.loop(0, 5)
    def _(tt):
        t = tt - 1

        @pl.when(tt < 3)
        def _():
            stage1(2 * tt + 2)

        @pl.when(tt < 4)
        def _():
            stage2(2 * tt)

        @pl.when(tt >= 1)
        def _():
            stage3(2 * tt - 1)

        @pl.when(tt == 0)
        def _():
            o_copy.wait()
            for p in range(1, nh):
                o_exchange(p).wait_recv()
            for lf in range(2):
                ot_ref[:, pl.ds(lf * TOKF, TOKF)] = o_ref[lf].astype(jnp.float32).T.astype(jnp.bfloat16)
            w_copy.wait()
            dacc[...] = jnp.zeros_like(dacc)

        @pl.when(tt == 4)
        def _():
            @pl.loop(0, heads)
            def _(hh):
                for i in range(3):
                    for p in order:
                        exchange(i, hh, p).start()

        @pl.when(tt >= 1)
        def _():
            s1_send[t] = one_chunk(2 * t).astype(jnp.bfloat16)
            s1(t).start()

        @pl.when(tt < 3)
        def _():
            stage1(2 * tt + 3)

        @pl.when(tt < 4)
        def _():
            stage2(2 * tt + 1)
            stage3(2 * tt)

        @pl.when(t == 2)
        def _():
            finish_near(0)

        @pl.when(t == 3)
        def _():
            finish_near(1)

        @pl.when(tt >= 1)
        def _():
            gsum[t] = one_chunk(2 * t + 1)
            s1(t).wait_recv()
            gsum[t] += s1_recv[t].astype(jnp.float32)

        @pl.when(t == 0)
        def _():
            for i in range(2):
                far_send[i] = gsum[0, pl.ds(320 * i, 320), :].astype(jnp.bfloat16)
                far(i).start()

    x_copy = pltpu.make_async_remote_copy(
        src_ref=x_send, dst_ref=x_recv, send_sem=x_ssem, recv_sem=x_rsem,
        device_id={"fsdp": 1 - s}, device_id_type=MESH,
    )

    def halo_grad(i, hh):
        return pltpu.make_async_remote_copy(
            src_ref=h_send.at[i, hh], dst_ref=h_recv.at[i, hh], send_sem=hg_ssem.at[i, hh], recv_sem=hg_rsem.at[i, hh],
            device_id={"frame": left if i == 0 else right}, device_id_type=MESH,
        )

    def bias_of(fr, column, offset):
        target = fr + offset
        inside = (target >= 0) & (target < 2 * nf)
        chosen = flags[column, fr] == 1
        first = jnp.where(inside, 0.0, NEG).astype(jnp.float32)
        second = jnp.where(inside & chosen, 0.0, NEG).astype(jnp.float32)
        return first, second

    def attend(hh):
        hs = pl.ds(pl.multiple_of(hh * HD, 128), HD)
        gk = []
        gv = []
        for lf in range(2):
            q = q_ref[hh, lf]
            parts = []
            for w in range(3):
                sc = dot(k_ref[hh, lf + w], q, NT) * (inv_root * LOG2E)
                if w == 1:
                    parts.append(sc)
                else:
                    first, second = bias_of(2 * f + lf, 0 if w == 0 else 1, w - 1)
                    parts.append(jnp.concatenate([sc[:128] + first, sc[128:] + second], axis=0))
            m = functools.reduce(jnp.maximum, [jnp.max(x, axis=0, keepdims=True) for x in parts])
            parts = [jnp.exp2(x - m) for x in parts]
            total = functools.reduce(jnp.add, [jnp.sum(x, axis=0, keepdims=True) for x in parts])
            inv = 1.0 / total
            d_out = dacc[pl.ds(lf * TOKF, TOKF), hs].astype(jnp.bfloat16)
            delta = jnp.sum(
                (d_out.astype(jnp.float32) * o_ref[lf, :, hs].astype(jnp.float32)).T, axis=0, keepdims=True
            )
            dq_t = jnp.zeros((HD, TOKF), jnp.float32)
            for w in range(3):
                pr = parts[w] * inv
                dp = dot(v_ref[hh, lf + w], d_out, NT)
                ds = (pr * (dp - delta)).astype(jnp.bfloat16)
                gv.append(dot(pr.astype(jnp.bfloat16), d_out, NN))
                gk.append(dot(ds, q, NN) * inv_root)
                kt = k_ref[hh, lf + w].astype(jnp.float32).T.astype(jnp.bfloat16)
                dq_t = dq_t + dot(kt, ds, NN)
            dq_ref[hh, lf] = (dq_t.T * inv_root).astype(jnp.bfloat16)
        h_send[0, hh, 0] = gk[0].astype(jnp.bfloat16)
        h_send[0, hh, 1] = gv[0].astype(jnp.bfloat16)
        h_send[1, hh, 0] = gk[5].astype(jnp.bfloat16)
        h_send[1, hh, 1] = gv[5].astype(jnp.bfloat16)
        halo_grad(0, hh).start()
        halo_grad(1, hh).start()
        own_k[hh, 0] = gk[1] + gk[3]
        own_k[hh, 1] = gk[2] + gk[4]
        own_v[hh, 0] = gv[1] + gv[3]
        own_v[hh, 1] = gv[2] + gv[4]

    def out_copy(i, hh):
        hs = pl.ds(pl.multiple_of(hh * HD, 128), HD)
        src, dst = ((dq_ref, dq_hbm), (dk_ref, dk_hbm), (dv_ref, dv_hbm))[i]
        return pltpu.make_async_copy(src.at[hh], dst.at[:, :, hs], out_sem.at[i, hh])

    def finish(hh):
        halo_grad(0, hh).wait_recv()
        halo_grad(1, hh).wait_recv()
        dk_ref[hh, 0] = (own_k[hh, 0] + h_recv[1, hh, 0].astype(jnp.float32)).astype(jnp.bfloat16)
        dk_ref[hh, 1] = (own_k[hh, 1] + h_recv[0, hh, 0].astype(jnp.float32)).astype(jnp.bfloat16)
        dv_ref[hh, 0] = (own_v[hh, 0] + h_recv[1, hh, 1].astype(jnp.float32)).astype(jnp.bfloat16)
        dv_ref[hh, 1] = (own_v[hh, 1] + h_recv[0, hh, 1].astype(jnp.float32)).astype(jnp.bfloat16)
        for i in range(3):
            out_copy(i, hh).start()

    @pl.loop(0, heads + 2)
    def _(n):
        @pl.when(n < heads)
        def _():
            for i in range(2):
                own_copy(i, n).wait()
                for p in range(1, nh):
                    exchange(i, n, p).wait_recv()
                halo(i, n, 0).start()
                halo(i, n, 1).start()

        @pl.when(n == heads)
        def _():
            near(0).wait_recv()
            near(1).wait_recv()
            gsum[3] += near_recv[0].astype(jnp.float32) + near_recv[1].astype(jnp.float32)
            x_send[...] = gsum[3, :, pl.ds(pl.multiple_of(256 * (1 - s), 128), 384)].astype(jnp.bfloat16)
            x_copy.start()

        @pl.when((n >= 1) & (n <= heads))
        def _():
            hh = n - 1
            own_copy(2, hh).wait()
            for p in range(1, nh):
                exchange(2, hh, p).wait_recv()
            for i in range(2):
                halo(i, hh, 0).wait_recv()
                halo(i, hh, 1).wait_recv()
            attend(hh)

        @pl.when(n >= 2)
        def _():
            finish(n - 2)

    x_copy.wait_recv()
    final = (gsum[3, :, pl.ds(pl.multiple_of(256 * s, 128), 384)] + x_recv[...].astype(jnp.float32)).T
    dw_ref[...] = jnp.where(s == 0, final[:320], final[64:384])
    dw_out = pltpu.make_async_copy(dw_ref, dw_hbm, dw_sem)
    dw_out.start()

    for p in range(1, nh):
        o_exchange(p).wait_send()

    @pl.loop(0, heads)
    def _(hh):
        for i in range(3):
            for p in range(1, nh):
                exchange(i, hh, p).wait_send()
            out_copy(i, hh).wait()
        for i in range(2):
            halo(i, hh, 0).wait_send()
            halo(i, hh, 1).wait_send()
            halo_grad(i, hh).wait_send()

    @pl.loop(0, 8)
    def _(t2):
        for idx in range(10):
            gather(t2, idx).wait_send()

    for i in range(2):
        far(i).wait_send()
        near(i).wait_send()

    @pl.loop(0, 4)
    def _(t):
        s1(t).wait_send()

    x_copy.wait_send()
    dw_out.wait()


def per_device(
    queries, key_rows, value_rows, saved_out, cotangent, out_weight, gate_table, levels, reach_flags
):
    frame_dev = queries.shape[1]
    tokens_all = lax.axis_size("fsdp") * frame_dev * lax.axis_size("frame") * TOKF
    bf, f32 = jnp.bfloat16, jnp.float32
    vm = pltpu.VMEM
    dma = pltpu.SemaphoreType.DMA
    hbm = pl.BlockSpec(memory_space=pl.ANY)
    smem = pl.BlockSpec(memory_space=pltpu.SMEM)
    out = jax.ShapeDtypeStruct((2, TOKF, 640), bf)
    dq, dk, dv, dw = pl.pallas_call(
        functools.partial(kernel, tokens_all),
        out_shape=(out, out, out, jax.ShapeDtypeStruct((320, 640), f32)),
        in_specs=[smem, smem] + [hbm] * 7,
        out_specs=(hbm,) * 4,
        scratch_shapes=[
            vm((640, 5120), bf),
            vm((2, TOKF, 5120), bf),
            vm((5, 2, TOKF, HD), bf),
            vm((2, TOKF, 640), bf),
            vm((5, 4, TOKF, HD), bf),
            vm((5, 4, TOKF, HD), bf),
            vm((2, 32, 5120), bf),
            vm((LEVELS, 5120), f32),
            vm((640, 2 * TOKF), bf),
            vm((2 * TOKF, 640), f32),
            vm((4, 640, 640), bf),
            vm((4, 640, 640), bf),
            vm((4, 640, 640), f32),
            vm((2, 320, 640), bf),
            vm((2, 320, 640), bf),
            vm((2, 640, 640), bf),
            vm((2, 640, 640), bf),
            vm((640, 384), bf),
            vm((640, 384), bf),
            vm((320, 640), f32),
            vm((5, 2, TOKF, HD), f32),
            vm((5, 2, TOKF, HD), f32),
            vm((2, 5, 2, TOKF, HD), bf),
            vm((2, 5, 2, TOKF, HD), bf),
            vm((5, 2, TOKF, HD), bf),
            vm((5, 2, TOKF, HD), bf),
            vm((5, 2, TOKF, HD), bf),
            dma((4,)),
            dma((8,)), dma((8,)),
            dma((5, 3, 8)), dma((5, 3, 8)),
            dma((8, 10)), dma((8, 10)),
            dma((2, 5, 2)), dma((2, 5, 2)),
            dma((4,)), dma((4,)),
            dma((2,)), dma((2,)),
            dma((2,)), dma((2,)),
            dma(()), dma(()),
            dma((2, 5)), dma((2, 5)),
            dma((3, 5)), dma(()),
        ],
        compiler_params=pltpu.CompilerParams(
            collective_id=0, has_side_effects=True, vmem_limit_bytes=67043328
        ),
        name="window_backward",
    )(
        reach_flags.T, levels, queries[0], key_rows[0], value_rows[0], saved_out[0], cotangent[0], out_weight, gate_table
    )
    return (dq[None], dk[None], dv[None], dw.T)


def solution(mesh):
    in_specs = (
        P("fsdp", "frame", "head", None),
        P("fsdp", "frame", "head", None),
        P("fsdp", "frame", "head", None),
        P("fsdp", "frame", "head", None),
        P("fsdp", "frame", "head", None),
        P("head", None),
        P(),
        P("frame"),
        P(),
    )
    out_specs = (
        P("fsdp", "frame", None, "head"),
        P("fsdp", "frame", None, "head"),
        P("fsdp", "frame", None, "head"),
        P("head", ("frame", "fsdp")),
    )
    return jax.shard_map(
        per_device, mesh=mesh, in_specs=in_specs, out_specs=out_specs, check_vma=False
    )
```

```python
import functools

import jax
import jax.numpy as jnp
from jax import lax
from jax.experimental import pallas as pl
from jax.experimental.pallas import tpu as pltpu
from jax.sharding import PartitionSpec as P

HD = 128
LEVELS = 64
TOKF = 256
NEG = -1e30
LOG2E = 1.4426950408889634
MESH = pl.DeviceIdType.MESH

NT = (((1,), (1,)), ((), ()))
NN = (((1,), (0,)), ((), ()))


def dot(a, b, dims):
    return lax.dot_general(a, b, dims, preferred_element_type=jnp.float32)


def kernel(
    tokens_all, flags, levels,
    q_hbm, k_hbm, v_hbm, o_hbm, c_hbm, w_hbm, gate_hbm,
    dq_ref, dk_ref, dv_ref, dw_ref,
    w_ref, g_ref, q_ref, o_ref, k_ref, v_ref, c_ref, gate_ref, ot_ref, dacc,
    s1_send, s1_recv, gsum, far_send, far_recv, near_send, near_recv, x_send, x_recv,
    own_k, own_v, h_send, h_recv,
    loc_sem, w_sem, exo_send, exo_recv, ex_send, ex_recv, ag_send, ag_recv, halo_ssem, halo_rsem,
    s1_ssem, s1_rsem, far_ssem, far_rsem, near_ssem, near_rsem, x_ssem, x_rsem, hg_ssem, hg_rsem,
):
    f, h, s = lax.axis_index("frame"), lax.axis_index("head"), lax.axis_index("fsdp")
    nf = 8
    nh = 8
    y, c = f // 2, f % 2
    xh, z = h // 4, h % 4
    zp, zm = (z + 1) % 4, (z + 3) % 4
    right, left = (f + 1) % nf, (f + 7) % nf
    up, down = (f + 2) % nf, (f + 6) % nf
    pair = 2 * y + 1 - c
    rows = 32
    wid = 640
    heads = 5
    inv_root = HD ** (-0.5)

    def col(j):
        return pl.ds(pl.multiple_of(j * wid, 128), wid)

    def rows_of(n):
        return pl.ds(pl.multiple_of(n * rows, 32), rows)

    my_rows = rows_of(h)

    def pieces(t2):
        core = 1 - c if t2 % 2 == 0 else c
        ahead, back = ((y + 1) % 4 * 2 + core) * wid, ((y + 3) % 4 * 2 + core) * wid
        return (
            ((((y + 2) % 4 * 2 + core) * wid, 0, wid),),
            ((ahead, 0, 384), (back, 384, 256)),
            ((ahead + 384, 0, 256), (back + 256, 256, 384)),
            (((y * 2 + core) * wid, 0, wid),),
        )[t2 // 2]

    def head_cols(d, hh):
        return pl.ds(pl.multiple_of(d * wid + hh * HD, 128), HD)

    c_copy = pltpu.make_async_copy(c_hbm, c_ref, loc_sem.at[0])
    gate_copy = pltpu.make_async_copy(gate_hbm, gate_ref, loc_sem.at[1])
    o_copy = pltpu.make_async_copy(o_hbm.at[:, :, col(h)], o_ref.at[:, my_rows, :], loc_sem.at[2])
    w_copies = []
    for t2 in range(8):
        for k, (start, at, width) in enumerate(pieces(t2)):
            w_copies.append(
                pltpu.make_async_copy(
                    w_hbm.at[:, pl.ds(pl.multiple_of(start, 128), width)], w_ref.at[t2, :, pl.ds(at, width)], w_sem.at[t2, k]
                )
            )

    def own_copy(i, hh):
        src, dst = (
            (k_hbm, k_ref.at[hh, pl.ds(1, 2), my_rows, :]),
            (v_hbm, v_ref.at[hh, pl.ds(1, 2), my_rows, :]),
            (q_hbm, q_ref.at[hh, :, my_rows, :]),
        )[i]
        return pltpu.make_async_copy(src.at[:, :, head_cols(h, hh)], dst, ex_recv.at[hh, i, 0])

    barrier = pltpu.get_barrier_semaphore()
    for p in range(1, nh):
        pl.semaphore_signal(barrier, inc=1, device_id={"head": (h + p) % nh}, device_id_type=MESH)
    for other in (right, left, up, down):
        pl.semaphore_signal(barrier, inc=1, device_id={"frame": other}, device_id_type=MESH)
    pl.semaphore_signal(barrier, inc=1, device_id={"fsdp": 1 - s}, device_id_type=MESH)
    c_copy.start()
    gate_copy.start()
    o_copy.start()
    for copy in w_copies:
        copy.start()

    @pl.loop(0, heads)
    def _(hh):
        for i in range(3):
            own_copy(i, hh).start()

    c_copy.wait()
    gate_copy.wait()
    for t2 in range(8):
        for start, at, width in pieces(t2):
            cols = pl.ds(pl.multiple_of(start, 128), width)
            for lf in range(2):
                gain = gate_ref[pl.ds(levels[lf], 1), cols]
                g_ref[t2, lf, my_rows, pl.ds(at, width)] = (c_ref[lf, :, cols].astype(jnp.float32) * gain).astype(jnp.bfloat16)
    pl.semaphore_wait(barrier, nh - 1 + 5)

    def o_exchange(p):
        d = (h + p) % nh
        return pltpu.make_async_remote_copy(
            src_ref=o_hbm.at[:, :, col(d)], dst_ref=o_ref.at[:, my_rows, :],
            send_sem=exo_send.at[p], recv_sem=exo_recv.at[p],
            device_id={"head": d}, device_id_type=MESH,
        )

    def exchange(i, hh, p):
        d = (h + p) % nh
        src, dst = (
            (k_hbm, k_ref.at[hh, pl.ds(1, 2), my_rows, :]),
            (v_hbm, v_ref.at[hh, pl.ds(1, 2), my_rows, :]),
            (q_hbm, q_ref.at[hh, :, my_rows, :]),
        )[i]
        return pltpu.make_async_remote_copy(
            src_ref=src.at[:, :, head_cols(d, hh)], dst_ref=dst,
            send_sem=ex_send.at[hh, i, p], recv_sem=ex_recv.at[hh, i, p],
            device_id={"head": d}, device_id_type=MESH,
        )

    def part(t2, n, half, idx, xt, zt):
        ref = g_ref.at[t2, :, rows_of(n)] if half is None else g_ref.at[t2, half, rows_of(n)]
        return pltpu.make_async_remote_copy(
            src_ref=ref, dst_ref=ref, send_sem=ag_send.at[t2, idx], recv_sem=ag_recv.at[t2, idx],
            device_id={"head": xt * 4 + zt}, device_id_type=MESH,
        )

    def gather(t2, idx):
        xo = 1 - xh
        return (
            lambda: part(t2, h, None, 0, xh, zp),
            lambda: part(t2, h, None, 1, xh, zm),
            lambda: part(t2, xh * 4 + zm, None, 2, xo, z),
            lambda: part(t2, xh * 4 + zp, None, 3, xo, z),
            lambda: part(t2, xh * 4 + zm, 0, 4, xh, zp),
            lambda: part(t2, xh * 4 + zp, 1, 5, xh, zm),
            lambda: part(t2, xo * 4 + zm, 0, 6, xh, zp),
            lambda: part(t2, xo * 4 + zm, 0, 7, xh, zm),
            lambda: part(t2, xo * 4 + zp, 1, 8, xh, zp),
            lambda: part(t2, xo * 4 + zp, 1, 9, xh, zm),
        )[idx]()

    def stage1(t2):
        gather(t2, 0).start()
        gather(t2, 1).start()

    def stage2(t2):
        gather(t2, 0).wait_recv()
        gather(t2, 2).start()
        gather(t2, 4).start()
        gather(t2, 1).wait_recv()
        gather(t2, 3).start()
        gather(t2, 5).start()

    def stage3(t2):
        gather(t2, 2).wait_recv()
        gather(t2, 6).start()
        gather(t2, 7).start()
        gather(t2, 3).wait_recv()
        gather(t2, 8).start()
        gather(t2, 9).start()

    order = (4, 2, 6, 1, 7, 3, 5)
    for t2 in range(4):
        stage1(t2)
    for p in order:
        o_exchange(p).start()

    def halo(i, hh, which):
        ref = (k_ref, v_ref)[i]
        return pltpu.make_async_remote_copy(
            src_ref=ref.at[hh, 2 if which == 0 else 1], dst_ref=ref.at[hh, 0 if which == 0 else 3],
            send_sem=halo_ssem.at[i, hh, which], recv_sem=halo_rsem.at[i, hh, which],
            device_id={"frame": right if which == 0 else left}, device_id_type=MESH,
        )

    def s1(t):
        return pltpu.make_async_remote_copy(
            src_ref=s1_send.at[t], dst_ref=s1_recv.at[t], send_sem=s1_ssem.at[t], recv_sem=s1_rsem.at[t],
            device_id={"frame": pair}, device_id_type=MESH,
        )

    far_cols = (pl.ds(0, 384), pl.ds(384, 256))
    near_cols = ((pl.ds(0, 384), pl.ds(384, 256)), (pl.ds(0, 256), pl.ds(256, 384)))

    def far(i):
        return pltpu.make_async_remote_copy(
            src_ref=far_send.at[:, far_cols[i]], dst_ref=far_recv.at[:, far_cols[i]],
            send_sem=far_ssem.at[i], recv_sem=far_rsem.at[i],
            device_id={"frame": up if i == 0 else down}, device_id_type=MESH,
        )

    def near(i, r):
        return pltpu.make_async_remote_copy(
            src_ref=near_send.at[i, :, near_cols[i][r]], dst_ref=near_recv.at[i, :, near_cols[i][r]],
            send_sem=near_ssem.at[i, r], recv_sem=near_rsem.at[i, r],
            device_id={"frame": up if i == 0 else down}, device_id_type=MESH,
        )

    def one_chunk(t2):
        for idx in range(4, 10):
            gather(t2, idx).wait_recv()
        rhs = g_ref[t2].reshape(2 * TOKF, wid)
        dacc[...] += dot(rhs, w_ref[t2], NT)
        return dot(ot_ref[...], rhs, NN) * (1.0 / tokens_all)

    def send_near(i, r):
        if (i, r) == (0, 0):
            far(0).wait_recv()
            near_send[0, :, pl.ds(0, 384)] = (gsum[1, :, pl.ds(0, 384)] + far_recv[:, pl.ds(0, 384)].astype(jnp.float32)).astype(
                jnp.bfloat16
            )
        elif (i, r) == (1, 0):
            near_send[1, :, pl.ds(0, 256)] = gsum[1, :, pl.ds(384, 256)].astype(jnp.bfloat16)
        elif (i, r) == (0, 1):
            near_send[0, :, pl.ds(384, 256)] = gsum[2, :, pl.ds(0, 256)].astype(jnp.bfloat16)
        else:
            far(1).wait_recv()
            near_send[1, :, pl.ds(256, 128)] = gsum[2, :, pl.ds(256, 128)].astype(jnp.bfloat16)
            near_send[1, :, pl.ds(384, 256)] = (gsum[2, :, pl.ds(384, 256)] + far_recv[:, pl.ds(384, 256)].astype(jnp.float32)).astype(
                jnp.bfloat16
            )
        near(i, r).start()

    def send_head(n):
        @pl.when(n < heads)
        def _():
            for i in range(2):
                for p in order:
                    exchange(i, n, p).start()

        @pl.when((n >= 1) & (n <= heads))
        def _():
            for p in order:
                exchange(2, n - 1, p).start()

    def forward(tt, u):
        @pl.when(tt < 4)
        def _():
            stage3(u)

        @pl.when(tt < 3)
        def _():
            stage2(u + 2)

        @pl.when(tt < 2)
        def _():
            stage1(u + 4)

    stage2(0)
    stage2(1)

    @pl.loop(0, 5)
    def _(tt):
        t = tt - 1

        forward(tt, 2 * tt)

        @pl.when(tt == 0)
        def _():
            o_copy.wait()
            for p in range(1, nh):
                o_exchange(p).wait_recv()
            for lf in range(2):
                ot_ref[:, pl.ds(lf * TOKF, TOKF)] = o_ref[lf].astype(jnp.float32).T.astype(jnp.bfloat16)
            for copy in w_copies:
                copy.wait()
            dacc[...] = jnp.zeros_like(dacc)

        @pl.when(tt >= 1)
        def _():
            s1_send[t] = one_chunk(2 * t).astype(jnp.bfloat16)
            s1(t).start()

        forward(tt, 2 * tt + 1)

        @pl.when(tt == 3)
        def _():
            for n in range(3):
                send_head(n)

        @pl.when(t == 2)
        def _():
            send_near(0, 0)

        @pl.when(tt >= 1)
        def _():
            gsum[t] = one_chunk(2 * t + 1)
            s1(t).wait_recv()
            gsum[t] += s1_recv[t].astype(jnp.float32)

        @pl.when(t == 0)
        def _():
            for i in range(2):
                far_send[:, far_cols[i]] = gsum[0, :, far_cols[i]].astype(jnp.bfloat16)
                far(i).start()

        @pl.when(t == 1)
        def _():
            send_near(1, 0)

        @pl.when(t == 2)
        def _():
            send_near(0, 1)
            send_near(1, 1)

    x_copy = pltpu.make_async_remote_copy(
        src_ref=x_send, dst_ref=x_recv, send_sem=x_ssem, recv_sem=x_rsem,
        device_id={"fsdp": 1 - s}, device_id_type=MESH,
    )

    def own_block():
        for i in range(2):
            for r in range(2):
                near(i, r).wait_recv()
        total = gsum[3] + near_recv[0].astype(jnp.float32) + near_recv[1].astype(jnp.float32)
        gsum[0] = total.T
        x_send[...] = gsum[0, pl.ds(pl.multiple_of(320 * (1 - s), 64), 320), :].astype(jnp.bfloat16)
        x_copy.start()

    def halo_grad(i, hh):
        return pltpu.make_async_remote_copy(
            src_ref=h_send.at[i, hh], dst_ref=h_recv.at[i, hh], send_sem=hg_ssem.at[i, hh], recv_sem=hg_rsem.at[i, hh],
            device_id={"frame": left if i == 0 else right}, device_id_type=MESH,
        )

    def bias_of(fr, column, offset):
        target = fr + offset
        inside = (target >= 0) & (target < 2 * nf)
        chosen = flags[column, fr] == 1
        first = jnp.where(inside, 0.0, NEG).astype(jnp.float32)
        second = jnp.where(inside & chosen, 0.0, NEG).astype(jnp.float32)
        return first, second

    def attend(hh):
        hs = pl.ds(pl.multiple_of(hh * HD, 128), HD)
        for lf in range(2):
            q = q_ref[hh, lf]
            parts = []
            for w in range(3):
                sc = dot(k_ref[hh, lf + w], q, NT) * (inv_root * LOG2E)
                if w == 1:
                    parts.append(sc)
                else:
                    first, second = bias_of(2 * f + lf, 0 if w == 0 else 1, w - 1)
                    parts.append(jnp.concatenate([sc[:128] + first, sc[128:] + second], axis=0))
            m = functools.reduce(jnp.maximum, [jnp.max(x, axis=0, keepdims=True) for x in parts])
            parts = [jnp.exp2(x - m) for x in parts]
            total = functools.reduce(jnp.add, [jnp.sum(x, axis=0, keepdims=True) for x in parts])
            inv = 1.0 / total
            d_out = dacc[pl.ds(lf * TOKF, TOKF), hs].astype(jnp.bfloat16)
            delta = jnp.sum(
                (d_out.astype(jnp.float32) * o_ref[lf, :, hs].astype(jnp.float32)).T, axis=0, keepdims=True
            )
            dq_t = jnp.zeros((HD, TOKF), jnp.float32)
            for w in (0, 1, 2) if lf == 0 else (2, 1, 0):
                pr = parts[w] * inv
                dp = dot(v_ref[hh, lf + w], d_out, NT)
                ds = (pr * (dp - delta)).astype(jnp.bfloat16)
                gv = dot(pr.astype(jnp.bfloat16), d_out, NN)
                gk = dot(ds, q, NN) * inv_root
                slot = lf + w
                if slot in (0, 3):
                    h_send[slot // 3, hh, 0] = gk.astype(jnp.bfloat16)
                    h_send[slot // 3, hh, 1] = gv.astype(jnp.bfloat16)
                    halo_grad(slot // 3, hh).start()
                elif lf == 0:
                    own_k[hh, slot - 1] = gk
                    own_v[hh, slot - 1] = gv
                else:
                    own_k[hh, slot - 1] += gk
                    own_v[hh, slot - 1] += gv
                kt = k_ref[hh, lf + w].astype(jnp.float32).T.astype(jnp.bfloat16)
                dq_t = dq_t + dot(kt, ds, NN)
            dq_ref[lf, :, hs] = (dq_t.T * inv_root).astype(jnp.bfloat16)

    def finish(hh):
        hs = pl.ds(pl.multiple_of(hh * HD, 128), HD)
        halo_grad(0, hh).wait_recv()
        halo_grad(1, hh).wait_recv()
        dk_ref[0, :, hs] = (own_k[hh, 0] + h_recv[1, hh, 0].astype(jnp.float32)).astype(jnp.bfloat16)
        dk_ref[1, :, hs] = (own_k[hh, 1] + h_recv[0, hh, 0].astype(jnp.float32)).astype(jnp.bfloat16)
        dv_ref[0, :, hs] = (own_v[hh, 0] + h_recv[1, hh, 1].astype(jnp.float32)).astype(jnp.bfloat16)
        dv_ref[1, :, hs] = (own_v[hh, 1] + h_recv[0, hh, 1].astype(jnp.float32)).astype(jnp.bfloat16)

    @pl.loop(0, heads + 2)
    def _(n):
        @pl.when(n < heads)
        def _():
            for i in range(2):
                own_copy(i, n).wait()
                for p in range(1, nh):
                    exchange(i, n, p).wait_recv()
                halo(i, n, 0).start()
                halo(i, n, 1).start()

        @pl.when(n == 3)
        def _():
            own_block()

        send_head(n + 3)

        @pl.when((n >= 1) & (n <= heads))
        def _():
            hh = n - 1
            own_copy(2, hh).wait()
            for p in range(1, nh):
                exchange(2, hh, p).wait_recv()
            for i in range(2):
                halo(i, hh, 0).wait_recv()
                halo(i, hh, 1).wait_recv()
            attend(hh)

        @pl.when(n >= 2)
        def _():
            finish(n - 2)

    x_copy.wait_recv()
    dw_ref[...] = gsum[0, pl.ds(pl.multiple_of(320 * s, 64), 320), :] + x_recv[...].astype(jnp.float32)

    for p in range(1, nh):
        o_exchange(p).wait_send()

    @pl.loop(0, heads)
    def _(hh):
        for i in range(3):
            for p in range(1, nh):
                exchange(i, hh, p).wait_send()
        for i in range(2):
            halo(i, hh, 0).wait_send()
            halo(i, hh, 1).wait_send()
            halo_grad(i, hh).wait_send()

    @pl.loop(0, 8)
    def _(t2):
        for idx in range(10):
            gather(t2, idx).wait_send()

    for i in range(2):
        far(i).wait_send()
        near(i, 0).wait_send()
        near(i, 1).wait_send()
    x_copy.wait_send()

    @pl.loop(0, 4)
    def _(t):
        s1(t).wait_send()


def write_out(*refs):
    copies = [pltpu.make_async_copy(refs[i], refs[4 + i], refs[8].at[i]) for i in range(4)]
    for copy in copies:
        copy.start()
    for copy in copies:
        copy.wait()


def per_device(
    queries, key_rows, value_rows, saved_out, cotangent, out_weight, gate_table, levels, reach_flags
):
    frame_dev = queries.shape[1]
    tokens_all = lax.axis_size("fsdp") * frame_dev * lax.axis_size("frame") * TOKF
    bf, f32 = jnp.bfloat16, jnp.float32
    vm = pltpu.VMEM
    dma = pltpu.SemaphoreType.DMA
    hbm = pl.BlockSpec(memory_space=pl.ANY)
    smem = pl.BlockSpec(memory_space=pltpu.SMEM)
    out = vm((2, TOKF, 640), bf)
    held = pl.pallas_call(
        functools.partial(kernel, tokens_all),
        out_shape=(out, out, out, vm((320, 640), f32)),
        in_specs=[smem, smem] + [hbm] * 7,
        out_specs=(pl.BlockSpec(memory_space=vm),) * 4,
        scratch_shapes=[
            vm((8, 640, 640), bf),
            vm((8, 2, TOKF, 640), bf),
            vm((5, 2, TOKF, HD), bf),
            vm((2, TOKF, 640), bf),
            vm((5, 4, TOKF, HD), bf),
            vm((5, 4, TOKF, HD), bf),
            vm((2, 32, 5120), bf),
            vm((LEVELS, 5120), f32),
            vm((640, 2 * TOKF), bf),
            vm((2 * TOKF, 640), f32),
            vm((4, 640, 640), bf),
            vm((4, 640, 640), bf),
            vm((4, 640, 640), f32),
            vm((640, 640), bf),
            vm((640, 640), bf),
            vm((2, 640, 640), bf),
            vm((2, 640, 640), bf),
            vm((320, 640), bf),
            vm((320, 640), bf),
            vm((5, 2, TOKF, HD), f32),
            vm((5, 2, TOKF, HD), f32),
            vm((2, 5, 2, TOKF, HD), bf),
            vm((2, 5, 2, TOKF, HD), bf),
            dma((3,)), dma((8, 2)),
            dma((8,)), dma((8,)),
            dma((5, 3, 8)), dma((5, 3, 8)),
            dma((8, 10)), dma((8, 10)),
            dma((2, 5, 2)), dma((2, 5, 2)),
            dma((4,)), dma((4,)),
            dma((2,)), dma((2,)),
            dma((2, 2)), dma((2, 2)),
            dma(()), dma(()),
            dma((2, 5)), dma((2, 5)),
        ],
        compiler_params=pltpu.CompilerParams(
            collective_id=0, has_side_effects=True, vmem_limit_bytes=58 * 2**20
        ),
        name="window_backward",
    )(
        reach_flags.T, levels, queries[0], key_rows[0], value_rows[0], saved_out[0], cotangent[0], out_weight, gate_table
    )
    out = jax.ShapeDtypeStruct((2, TOKF, 640), bf)
    dq, dk, dv, dw = pl.pallas_call(
        write_out,
        out_shape=(out, out, out, jax.ShapeDtypeStruct((320, 640), f32)),
        in_specs=[pl.BlockSpec(memory_space=vm)] * 4,
        out_specs=(hbm,) * 4,
        scratch_shapes=[dma((4,))],
        compiler_params=pltpu.CompilerParams(vmem_limit_bytes=4 * 2**20),
        name="write_out",
    )(*held)
    return (dq[None], dk[None], dv[None], dw.T)


def solution(mesh):
    in_specs = (
        P("fsdp", "frame", "head", None),
        P("fsdp", "frame", "head", None),
        P("fsdp", "frame", "head", None),
        P("fsdp", "frame", "head", None),
        P("fsdp", "frame", "head", None),
        P("head", None),
        P(),
        P("frame"),
        P(),
    )
    out_specs = (
        P("fsdp", "frame", None, "head"),
        P("fsdp", "frame", None, "head"),
        P("fsdp", "frame", None, "head"),
        P("head", ("frame", "fsdp")),
    )
    return jax.shard_map(
        per_device, mesh=mesh, in_specs=in_specs, out_specs=out_specs, check_vma=False
    )
```

```python
import functools

import jax
import jax.numpy as jnp
from jax import lax
from jax.experimental import pallas as pl
from jax.experimental.pallas import tpu as pltpu
from jax.sharding import PartitionSpec as P

HD = 128
LEVELS = 64
TOKF = 256
NEG = -1e30
LOG2E = 1.4426950408889634
MESH = pl.DeviceIdType.MESH

NT = (((1,), (1,)), ((), ()))
NN = (((1,), (0,)), ((), ()))


def dot(a, b, dims):
    return lax.dot_general(a, b, dims, preferred_element_type=jnp.float32)


def kernel(
    tokens_all, flags, levels,
    q_hbm, k_hbm, v_hbm, o_hbm, c_hbm, w_hbm, gate_hbm,
    dq_ref, dk_ref, dv_ref, dw_ref,
    w_ref, g_ref, q_ref, o_ref, k_ref, v_ref, gate_ref, gain_ref, ot_ref, dacc,
    s1_send, s1_recv, gsum, far_send, far_recv, near_send, near_recv, x_send, x_recv,
    own_k, own_v, h_send, h_recv,
    loc_sem, w_sem, c_sem, own_sem, exo_send, exo_recv, ex_send, ex_recv, ag_send, ag_recv, ag_part, halo_ssem, halo_rsem,
    s1_ssem, s1_rsem, far_ssem, far_rsem, near_ssem, near_rsem, x_ssem, x_rsem, hg_ssem, hg_rsem,
):
    f, h, s = lax.axis_index("frame"), lax.axis_index("head"), lax.axis_index("fsdp")
    nf = 8
    nh = 8
    y, c = f // 2, f % 2
    xh, z = h // 4, h % 4
    zp, zm = (z + 1) % 4, (z + 3) % 4
    right, left = (f + 1) % nf, (f + 7) % nf
    up, down = (f + 2) % nf, (f + 6) % nf
    pair = 2 * y + 1 - c
    rows = 32
    wid = 640
    heads = 5
    inv_root = HD ** (-0.5)

    def col(j):
        return pl.ds(pl.multiple_of(j * wid, 128), wid)

    def rows_of(n):
        return pl.ds(pl.multiple_of(n * rows, 32), rows)

    my_rows = rows_of(h)

    def pieces(t2):
        core = 1 - c if t2 % 2 == 0 else c
        ahead, back = ((y + 1) % 4 * 2 + core) * wid, ((y + 3) % 4 * 2 + core) * wid
        return (
            ((((y + 2) % 4 * 2 + core) * wid, 0, wid),),
            ((ahead, 0, 384), (back + 384, 384, 256)),
            ((ahead + 384, 0, 256), (back, 256, 384)),
            (((y * 2 + core) * wid, 0, wid),),
        )[t2 // 2]

    def head_cols(d, hh):
        return pl.ds(pl.multiple_of(d * wid + hh * HD, 128), HD)

    c_copies = []
    for t2 in range(8):
        for k, (start, at, width) in enumerate(pieces(t2)):
            c_copies.append(
                pltpu.make_async_copy(
                    c_hbm.at[:, :, pl.ds(pl.multiple_of(start, 128), width)],
                    g_ref.at[t2, :, my_rows, pl.ds(at, width)],
                    c_sem,
                )
            )
    gate_copy = pltpu.make_async_copy(gate_hbm, gate_ref, loc_sem.at[1])
    o_copy = pltpu.make_async_copy(o_hbm.at[:, :, col(h)], o_ref.at[:, my_rows, :], loc_sem.at[2])
    w_copies = []
    for t2 in range(8):
        for k, (start, at, width) in enumerate(pieces(t2)):
            w_copies.append(
                pltpu.make_async_copy(
                    w_hbm.at[:, pl.ds(pl.multiple_of(start, 128), width)], w_ref.at[t2, :, pl.ds(at, width)], w_sem
                )
            )

    def own_copy(i, hh):
        src, dst = (
            (k_hbm, k_ref.at[hh, pl.ds(1, 2), my_rows, :]),
            (v_hbm, v_ref.at[hh, pl.ds(1, 2), my_rows, :]),
            (q_hbm, q_ref.at[hh, :, my_rows, :]),
        )[i]
        return pltpu.make_async_copy(src.at[:, :, head_cols(h, hh)], dst, own_sem)

    barrier = pltpu.get_barrier_semaphore()
    for p in range(1, nh):
        pl.semaphore_signal(barrier, inc=1, device_id={"head": (h + p) % nh}, device_id_type=MESH)
    for other in (right, left, up, down):
        pl.semaphore_signal(barrier, inc=1, device_id={"frame": other}, device_id_type=MESH)
    pl.semaphore_signal(barrier, inc=1, device_id={"fsdp": 1 - s}, device_id_type=MESH)
    for copy in c_copies:
        copy.start()
    pl.semaphore_wait(barrier, nh - 1 + 5)

    def wait_bytes(ref, sem):
        pltpu.make_async_copy(ref, ref, sem).wait()

    def o_exchange(p):
        d = (h + p) % nh
        return pltpu.make_async_remote_copy(
            src_ref=o_hbm.at[:, :, col(d)], dst_ref=o_ref.at[:, my_rows, :],
            send_sem=exo_send, recv_sem=exo_recv,
            device_id={"head": d}, device_id_type=MESH,
        )

    def exchange(i, hh, p):
        d = (h + p) % nh
        src, dst = (
            (k_hbm, k_ref.at[hh, pl.ds(1, 2), my_rows, :]),
            (v_hbm, v_ref.at[hh, pl.ds(1, 2), my_rows, :]),
            (q_hbm, q_ref.at[hh, :, my_rows, :]),
        )[i]
        return pltpu.make_async_remote_copy(
            src_ref=src.at[:, :, head_cols(d, hh)], dst_ref=dst,
            send_sem=ex_send, recv_sem=ex_recv.at[hh, i // 2],
            device_id={"head": d}, device_id_type=MESH,
        )

    def part(t2, n, half, idx, xt, zt):
        ref = g_ref.at[t2, :, rows_of(n)] if half is None else g_ref.at[t2, half, rows_of(n)]
        return pltpu.make_async_remote_copy(
            src_ref=ref, dst_ref=ref, send_sem=ag_send, recv_sem=ag_recv.at[t2, idx // 2] if idx < 4 else ag_part.at[t2],
            device_id={"head": xt * 4 + zt}, device_id_type=MESH,
        )

    def gather(t2, idx):
        xo = 1 - xh
        return (
            lambda: part(t2, h, None, 0, xh, zp),
            lambda: part(t2, h, None, 1, xh, zm),
            lambda: part(t2, xh * 4 + zm, None, 2, xo, z),
            lambda: part(t2, xh * 4 + zp, None, 3, xo, z),
            lambda: part(t2, xh * 4 + zm, 0, 4, xh, zp),
            lambda: part(t2, xh * 4 + zp, 1, 5, xh, zm),
            lambda: part(t2, xo * 4 + zm, 0, 6, xh, zp),
            lambda: part(t2, xo * 4 + zm, 0, 7, xh, zm),
            lambda: part(t2, xo * 4 + zp, 1, 8, xh, zp),
            lambda: part(t2, xo * 4 + zp, 1, 9, xh, zm),
        )[idx]()

    def stage1(t2):
        gather(t2, 0).start()
        gather(t2, 1).start()

    def stage2(t2):
        wait_bytes(g_ref.at[t2, 0, pl.ds(0, 128)], ag_recv.at[t2, 0])
        for idx in range(2, 6):
            gather(t2, idx).start()

    def stage3(t2):
        wait_bytes(g_ref.at[t2, 0, pl.ds(0, 128)], ag_recv.at[t2, 1])
        for idx in range(6, 10):
            gather(t2, idx).start()

    order = (4, 2, 6, 1, 7, 3, 5)

    def halo(i, hh, which):
        ref = (k_ref, v_ref)[i]
        return pltpu.make_async_remote_copy(
            src_ref=ref.at[hh, 2 if which == 0 else 1], dst_ref=ref.at[hh, 0 if which == 0 else 3],
            send_sem=halo_ssem, recv_sem=halo_rsem.at[hh],
            device_id={"frame": right if which == 0 else left}, device_id_type=MESH,
        )

    def s1(t):
        return pltpu.make_async_remote_copy(
            src_ref=s1_send.at[t], dst_ref=s1_recv.at[t], send_sem=s1_ssem, recv_sem=s1_rsem.at[t],
            device_id={"frame": pair}, device_id_type=MESH,
        )

    far_cols = (pl.ds(384, 256), pl.ds(0, 384))
    near_cols = ((pl.ds(0, 384), pl.ds(384, 256)), (pl.ds(384, 256), pl.ds(0, 384)))

    def far(i):
        return pltpu.make_async_remote_copy(
            src_ref=far_send.at[:, far_cols[i]], dst_ref=far_recv.at[:, far_cols[i]],
            send_sem=far_ssem, recv_sem=far_rsem.at[i],
            device_id={"frame": up if i == 0 else down}, device_id_type=MESH,
        )

    def near(i, r):
        return pltpu.make_async_remote_copy(
            src_ref=near_send.at[i, :, near_cols[i][r]], dst_ref=near_recv.at[i, :, near_cols[i][r]],
            send_sem=near_ssem, recv_sem=near_rsem,
            device_id={"frame": up if i == 0 else down}, device_id_type=MESH,
        )

    def one_chunk(t2):
        wait_bytes(g_ref.at[t2, 0, pl.ds(0, 192)], ag_part.at[t2])
        gated = [
            (g_ref[t2, lf].astype(jnp.float32) * gain_ref[t2, pl.ds(lf, 1), :]).astype(jnp.bfloat16) for lf in range(2)
        ]
        rhs = jnp.concatenate(gated, axis=0)
        dacc[...] += dot(rhs, w_ref[t2], NT)
        return dot(ot_ref[...], rhs, NN) * (1.0 / tokens_all)

    def send_near(i, r):
        cols = near_cols[i][r]
        held = ((pl.ds(0, 384), pl.ds(0, 256)), (pl.ds(384, 256), pl.ds(256, 384)))[i][r]
        total = gsum[1 + r, :, held]
        if r == 1:
            far(i).wait_recv()
            total = total + far_recv[:, cols].astype(jnp.float32)
        near_send[i, :, cols] = total.astype(jnp.bfloat16)
        near(i, r).start()

    def send(names):
        for i, n in names:
            for p in order:
                exchange(i, n, p).start()

    for t2 in range(2):
        ((start, _, width),) = pieces(t2)
        for idx, to in ((0, zp), (1, zm)):
            pltpu.make_async_remote_copy(
                src_ref=c_hbm.at[:, :, pl.ds(pl.multiple_of(start, 128), width)], dst_ref=g_ref.at[t2, :, my_rows],
                send_sem=ag_send, recv_sem=ag_recv.at[t2, 0],
                device_id={"head": xh * 4 + to}, device_id_type=MESH,
            ).start()
    for p in order[:3]:
        o_exchange(p).start()
    o_copy.start()
    gate_copy.start()
    for copy in w_copies:
        copy.start()

    @pl.loop(0, heads)
    def _(hh):
        for i in range(3):
            own_copy(i, hh).start()

    stage2(0)
    pltpu.make_async_copy(g_ref.at[:, :, my_rows, :], g_ref.at[:, :, my_rows, :], c_sem).wait()
    stage2(1)
    for p in order[3:]:
        o_exchange(p).start()
    stage1(2)
    stage1(3)
    gate_copy.wait()
    for t2 in range(8):
        for start, at, width in pieces(t2):
            for lf in range(2):
                gain_ref[t2, pl.ds(lf, 1), pl.ds(at, width)] = gate_ref[
                    pl.ds(levels[lf], 1), pl.ds(pl.multiple_of(start, 128), width)
                ]

    def take(n):
        wait_bytes(k_ref.at[n, :, pl.ds(0, 224), :], ex_recv.at[n, 0])
        for i in range(2):
            halo(i, n, 0).start()
            halo(i, n, 1).start()

    def later(tt, u):
        @pl.when(tt < 3)
        def _():
            stage2(u + 2)

        @pl.when(tt < 2)
        def _():
            stage1(u + 4)

    @pl.loop(0, 5)
    def _(tt):
        t = tt - 1

        @pl.when(tt < 4)
        def _():
            stage3(2 * tt)

        later(tt, 2 * tt)

        @pl.when(tt >= 1)
        def _():
            gsum[t] = one_chunk(2 * t + 1)
            s1(t).wait_recv()
            gsum[t] += s1_recv[t].astype(jnp.float32)

        @pl.when(t == 0)
        def _():
            for i in range(2):
                far_send[:, far_cols[i]] = gsum[0, :, far_cols[i]].astype(jnp.bfloat16)
                far(i).start()

        @pl.when(t == 1)
        def _():
            send_near(0, 0)
            send_near(1, 0)

        @pl.when(t == 2)
        def _():
            send_near(0, 1)
            send_near(1, 1)

        @pl.when(tt < 4)
        def _():
            stage3(2 * tt + 1)

        later(tt, 2 * tt + 1)

        @pl.when(tt == 3)
        def _():
            send(((0, 0), (1, 0), (2, 0), (0, 1), (1, 1)))

        @pl.when(tt == 0)
        def _():
            o_copy.wait()
            wait_bytes(o_ref.at[:, pl.ds(0, 224), :], exo_recv)
            wait_bytes(o_ref.at[:, pl.ds(0, 224), :], exo_send)
            for lf in range(2):
                ot_ref[:, pl.ds(lf * TOKF, TOKF)] = o_ref[lf].astype(jnp.float32).T.astype(jnp.bfloat16)
            wait_bytes(w_ref, w_sem)
            wait_bytes(k_ref.at[0, :, pl.ds(0, 240), :], own_sem)
            dacc[...] = jnp.zeros_like(dacc)

        @pl.when(tt < 4)
        def _():
            s1_send[tt] = one_chunk(2 * tt).astype(jnp.bfloat16)
            s1(tt).start()

    send(((2, 1), (0, 2), (1, 2), (2, 2)))
    take(0)

    x_copy = pltpu.make_async_remote_copy(
        src_ref=x_send, dst_ref=x_recv, send_sem=x_ssem, recv_sem=x_rsem,
        device_id={"fsdp": 1 - s}, device_id_type=MESH,
    )

    def own_block():
        wait_bytes(near_recv, near_rsem)
        total = gsum[3] + near_recv[0].astype(jnp.float32) + near_recv[1].astype(jnp.float32)
        gsum[0] = total.T
        x_send[...] = gsum[0, pl.ds(pl.multiple_of(320 * (1 - s), 64), 320), :].astype(jnp.bfloat16)
        x_copy.start()

    def halo_grad(i, hh):
        return pltpu.make_async_remote_copy(
            src_ref=h_send.at[i, hh], dst_ref=h_recv.at[i, hh], send_sem=hg_ssem, recv_sem=hg_rsem.at[hh],
            device_id={"frame": left if i == 0 else right}, device_id_type=MESH,
        )

    def bias_of(fr, column, offset):
        target = fr + offset
        inside = (target >= 0) & (target < 2 * nf)
        chosen = flags[column, fr] == 1
        first = jnp.where(inside, 0.0, NEG).astype(jnp.float32)
        second = jnp.where(inside & chosen, 0.0, NEG).astype(jnp.float32)
        return first, second

    def attend(hh):
        hs = pl.ds(pl.multiple_of(hh * HD, 128), HD)
        for lf in range(2):
            q = q_ref[hh, lf]
            parts = []
            for w in range(3):
                sc = dot(k_ref[hh, lf + w], q, NT) * (inv_root * LOG2E)
                if w == 1:
                    parts.append(sc)
                else:
                    first, second = bias_of(2 * f + lf, 0 if w == 0 else 1, w - 1)
                    parts.append(jnp.concatenate([sc[:128] + first, sc[128:] + second], axis=0))
            m = functools.reduce(jnp.maximum, [jnp.max(x, axis=0, keepdims=True) for x in parts])
            parts = [jnp.exp2(x - m) for x in parts]
            total = functools.reduce(jnp.add, [jnp.sum(x, axis=0, keepdims=True) for x in parts])
            inv = 1.0 / total
            d_out = dacc[pl.ds(lf * TOKF, TOKF), hs].astype(jnp.bfloat16)
            delta = jnp.sum(
                (d_out.astype(jnp.float32) * o_ref[lf, :, hs].astype(jnp.float32)).T, axis=0, keepdims=True
            )
            dq_t = jnp.zeros((HD, TOKF), jnp.float32)
            for w in (0, 1, 2) if lf == 0 else (2, 1, 0):
                pr = parts[w] * inv
                dp = dot(v_ref[hh, lf + w], d_out, NT)
                ds = (pr * (dp - delta)).astype(jnp.bfloat16)
                gv = dot(pr.astype(jnp.bfloat16), d_out, NN)
                gk = dot(ds, q, NN) * inv_root
                slot = lf + w
                if slot in (0, 3):
                    h_send[slot // 3, hh, 0] = gk.astype(jnp.bfloat16)
                    h_send[slot // 3, hh, 1] = gv.astype(jnp.bfloat16)
                    halo_grad(slot // 3, hh).start()
                elif lf == 0:
                    own_k[hh, slot - 1] = gk
                    own_v[hh, slot - 1] = gv
                else:
                    own_k[hh, slot - 1] += gk
                    own_v[hh, slot - 1] += gv
                kt = k_ref[hh, lf + w].astype(jnp.float32).T.astype(jnp.bfloat16)
                dq_t = dq_t + dot(kt, ds, NN)
            dq_ref[lf, :, hs] = (dq_t.T * inv_root).astype(jnp.bfloat16)

    def finish(hh):
        hs = pl.ds(pl.multiple_of(hh * HD, 128), HD)
        wait_bytes(h_recv.at[:, hh], hg_rsem.at[hh])
        dk_ref[0, :, hs] = (own_k[hh, 0] + h_recv[1, hh, 0].astype(jnp.float32)).astype(jnp.bfloat16)
        dk_ref[1, :, hs] = (own_k[hh, 1] + h_recv[0, hh, 0].astype(jnp.float32)).astype(jnp.bfloat16)
        dv_ref[0, :, hs] = (own_v[hh, 0] + h_recv[1, hh, 1].astype(jnp.float32)).astype(jnp.bfloat16)
        dv_ref[1, :, hs] = (own_v[hh, 1] + h_recv[0, hh, 1].astype(jnp.float32)).astype(jnp.bfloat16)

    wait_bytes(g_ref.at[:, :, pl.ds(0, 224), :], ag_send)
    wait_bytes(s1_send, s1_ssem)
    wait_bytes(far_send, far_ssem)
    take(1)
    send(((0, 3), (1, 3), (0, 4), (1, 4), (2, 3), (2, 4)))

    @pl.loop(0, heads)
    def _(n):
        @pl.when((n >= 1) & (n <= 2))
        def _():
            take(n + 1)

        @pl.when(n == 1)
        def _():
            own_block()

        @pl.when(n == 2)
        def _():
            take(4)

        wait_bytes(q_ref.at[n, :, pl.ds(0, 224), :], ex_recv.at[n, 1])
        wait_bytes(k_ref.at[n], halo_rsem.at[n])
        attend(n)

        @pl.when(n >= 2)
        def _():
            finish(n - 2)

    finish(heads - 2)
    wait_bytes(g_ref.at[pl.ds(0, 3), :, pl.ds(0, 224), :], ex_send)
    wait_bytes(k_ref, halo_ssem)
    wait_bytes(near_send, near_ssem)
    x_copy.wait_send()
    x_copy.wait_recv()
    dw_ref[...] = gsum[0, pl.ds(pl.multiple_of(320 * s, 64), 320), :] + x_recv[...].astype(jnp.float32)
    finish(heads - 1)
    wait_bytes(h_send, hg_ssem)


def write_out(*refs):
    copies = [pltpu.make_async_copy(refs[i], refs[4 + i], refs[8].at[i]) for i in range(4)]
    for copy in copies:
        copy.start()
    for copy in copies:
        copy.wait()


def per_device(
    queries, key_rows, value_rows, saved_out, cotangent, out_weight, gate_table, levels, reach_flags
):
    frame_dev = queries.shape[1]
    tokens_all = lax.axis_size("fsdp") * frame_dev * lax.axis_size("frame") * TOKF
    bf, f32 = jnp.bfloat16, jnp.float32
    vm = pltpu.VMEM
    dma = pltpu.SemaphoreType.DMA
    hbm = pl.BlockSpec(memory_space=pl.ANY)
    smem = pl.BlockSpec(memory_space=pltpu.SMEM)
    out = vm((2, TOKF, 640), bf)
    held = pl.pallas_call(
        functools.partial(kernel, tokens_all),
        out_shape=(out, out, out, vm((320, 640), f32)),
        in_specs=[smem, smem] + [hbm] * 7,
        out_specs=(pl.BlockSpec(memory_space=vm),) * 4,
        scratch_shapes=[
            vm((8, 640, 640), bf),
            vm((8, 2, TOKF, 640), bf),
            vm((5, 2, TOKF, HD), bf),
            vm((2, TOKF, 640), bf),
            vm((5, 4, TOKF, HD), bf),
            vm((5, 4, TOKF, HD), bf),
            vm((LEVELS, 5120), f32),
            vm((8, 2, 640), f32),
            vm((640, 2 * TOKF), bf),
            vm((2 * TOKF, 640), f32),
            vm((4, 640, 640), bf),
            vm((4, 640, 640), bf),
            vm((4, 640, 640), f32),
            vm((640, 640), bf),
            vm((640, 640), bf),
            vm((2, 640, 640), bf),
            vm((2, 640, 640), bf),
            vm((320, 640), bf),
            vm((320, 640), bf),
            vm((5, 2, TOKF, HD), f32),
            vm((5, 2, TOKF, HD), f32),
            vm((2, 5, 2, TOKF, HD), bf),
            vm((2, 5, 2, TOKF, HD), bf),
            dma((3,)), dma(()), dma(()), dma(()),
            dma(()), dma(()),
            dma(()), dma((5, 2)),
            dma(()), dma((8, 2)), dma((8,)),
            dma(()), dma((5,)),
            dma(()), dma((4,)),
            dma(()), dma((2,)),
            dma(()), dma(()),
            dma(()), dma(()),
            dma(()), dma((5,)),
        ],
        compiler_params=pltpu.CompilerParams(
            collective_id=0, has_side_effects=True, vmem_limit_bytes=58 * 2**20
        ),
        name="window_backward",
    )(
        reach_flags.T, levels, queries[0], key_rows[0], value_rows[0], saved_out[0], cotangent[0], out_weight, gate_table
    )
    out = jax.ShapeDtypeStruct((2, TOKF, 640), bf)
    dq, dk, dv, dw = pl.pallas_call(
        write_out,
        out_shape=(out, out, out, jax.ShapeDtypeStruct((320, 640), f32)),
        in_specs=[pl.BlockSpec(memory_space=vm)] * 4,
        out_specs=(hbm,) * 4,
        scratch_shapes=[dma((4,))],
        compiler_params=pltpu.CompilerParams(vmem_limit_bytes=4 * 2**20),
        name="write_out",
    )(*held)
    return (dq[None], dk[None], dv[None], dw.T)


def solution(mesh):
    in_specs = (
        P("fsdp", "frame", "head", None),
        P("fsdp", "frame", "head", None),
        P("fsdp", "frame", "head", None),
        P("fsdp", "frame", "head", None),
        P("fsdp", "frame", "head", None),
        P("head", None),
        P(),
        P("frame"),
        P(),
    )
    out_specs = (
        P("fsdp", "frame", None, "head"),
        P("fsdp", "frame", None, "head"),
        P("fsdp", "frame", None, "head"),
        P("head", ("frame", "fsdp")),
    )
    return jax.shard_map(
        per_device, mesh=mesh, in_specs=in_specs, out_specs=out_specs, check_vma=False
    )
```

```python
import functools

import jax
import jax.numpy as jnp
from jax import lax
from jax.experimental import pallas as pl
from jax.experimental.pallas import tpu as pltpu
from jax.sharding import PartitionSpec as P

HD = 128
LEVELS = 64
TOKF = 256
NEG = -1e30
LOG2E = 1.4426950408889634
MESH = pl.DeviceIdType.MESH

NT = (((1,), (1,)), ((), ()))
NN = (((1,), (0,)), ((), ()))


def dot(a, b, dims):
    return lax.dot_general(a, b, dims, preferred_element_type=jnp.float32)


def kernel(
    tokens_all, flags, levels,
    q_hbm, k_hbm, v_hbm, o_hbm, c_hbm, w_hbm, gate_hbm,
    dq_ref, dk_ref, dv_ref, dw_ref,
    w_ref, g_ref, q_ref, o_ref, k_ref, v_ref, gate_ref, gain_ref, ot_ref, dacc,
    s1_send, s1_recv, gsum, far_send, far_recv, near_send, near_recv, x_send, x_recv,
    own_k, own_v, h_send, h_recv,
    loc_sem, w_sem, c_sem, own_sem, exo_send, exo_recv, ex_send, ex_recv, ag_send, ag_recv, ag_part, halo_ssem, halo_rsem,
    s1_ssem, s1_rsem, far_ssem, far_rsem, near_ssem, near_rsem, x_ssem, x_rsem, hg_ssem, hg_rsem,
):
    f, h, s = lax.axis_index("frame"), lax.axis_index("head"), lax.axis_index("fsdp")
    nf = 8
    nh = 8
    y, c = f // 2, f % 2
    xh, z = h // 4, h % 4
    zp, zm = (z + 1) % 4, (z + 3) % 4
    right, left = (f + 1) % nf, (f + 7) % nf
    up, down = (f + 2) % nf, (f + 6) % nf
    pair = 2 * y + 1 - c
    rows = 32
    wid = 640
    heads = 5
    inv_root = HD ** (-0.5)

    def col(j):
        return pl.ds(pl.multiple_of(j * wid, 128), wid)

    def rows_of(n):
        return pl.ds(pl.multiple_of(n * rows, 32), rows)

    my_rows = rows_of(h)

    def pieces(t2):
        core = 1 - c if t2 % 2 == 0 else c
        ahead, back = ((y + 1) % 4 * 2 + core) * wid, ((y + 3) % 4 * 2 + core) * wid
        return (
            ((((y + 2) % 4 * 2 + core) * wid, 0, wid),),
            ((ahead, 0, 384), (back + 384, 384, 256)),
            ((ahead + 384, 0, 256), (back, 256, 384)),
            (((y * 2 + core) * wid, 0, wid),),
        )[t2 // 2]

    def head_cols(d, hh):
        return pl.ds(pl.multiple_of(d * wid + hh * HD, 128), HD)

    c_copies = []
    for t2 in range(8):
        for k, (start, at, width) in enumerate(pieces(t2)):
            c_copies.append(
                pltpu.make_async_copy(
                    c_hbm.at[:, :, pl.ds(pl.multiple_of(start, 128), width)],
                    g_ref.at[t2, :, my_rows, pl.ds(at, width)],
                    c_sem,
                )
            )
    gate_copy = pltpu.make_async_copy(gate_hbm, gate_ref, loc_sem.at[1])
    o_copy = pltpu.make_async_copy(o_hbm.at[:, :, col(h)], o_ref.at[:, my_rows, :], loc_sem.at[2])
    w_copies = []
    for t2 in range(8):
        for k, (start, at, width) in enumerate(pieces(t2)):
            w_copies.append(
                pltpu.make_async_copy(
                    w_hbm.at[:, pl.ds(pl.multiple_of(start, 128), width)], w_ref.at[t2, :, pl.ds(at, width)], w_sem
                )
            )

    def own_copy(i, hh):
        src, dst = (
            (k_hbm, k_ref.at[hh, pl.ds(1, 2), my_rows, :]),
            (v_hbm, v_ref.at[hh, pl.ds(1, 2), my_rows, :]),
            (q_hbm, q_ref.at[hh, :, my_rows, :]),
        )[i]
        return pltpu.make_async_copy(src.at[:, :, head_cols(h, hh)], dst, own_sem)

    barrier = pltpu.get_barrier_semaphore()
    for p in range(1, nh):
        pl.semaphore_signal(barrier, inc=1, device_id={"head": (h + p) % nh}, device_id_type=MESH)
    for other in (right, left, up, down):
        pl.semaphore_signal(barrier, inc=1, device_id={"frame": other}, device_id_type=MESH)
    pl.semaphore_signal(barrier, inc=1, device_id={"fsdp": 1 - s}, device_id_type=MESH)
    for copy in c_copies:
        copy.start()
    pl.semaphore_wait(barrier, nh - 1 + 5)

    def wait_bytes(ref, sem):
        pltpu.make_async_copy(ref, ref, sem).wait()

    def o_exchange(p):
        d = (h + p) % nh
        return pltpu.make_async_remote_copy(
            src_ref=o_hbm.at[:, :, col(d)], dst_ref=o_ref.at[:, my_rows, :],
            send_sem=exo_send, recv_sem=exo_recv,
            device_id={"head": d}, device_id_type=MESH,
        )

    def exchange(i, hh, p):
        d = (h + p) % nh
        src, dst = (
            (k_hbm, k_ref.at[hh, pl.ds(1, 2), my_rows, :]),
            (v_hbm, v_ref.at[hh, pl.ds(1, 2), my_rows, :]),
            (q_hbm, q_ref.at[hh, :, my_rows, :]),
        )[i]
        return pltpu.make_async_remote_copy(
            src_ref=src.at[:, :, head_cols(d, hh)], dst_ref=dst,
            send_sem=ex_send, recv_sem=ex_recv.at[hh, i // 2],
            device_id={"head": d}, device_id_type=MESH,
        )

    def part(t2, n, half, idx, xt, zt):
        ref = g_ref.at[t2, :, rows_of(n)] if half is None else g_ref.at[t2, half, rows_of(n)]
        return pltpu.make_async_remote_copy(
            src_ref=ref, dst_ref=ref, send_sem=ag_send, recv_sem=ag_recv.at[t2, idx // 2] if idx < 4 else ag_part.at[t2],
            device_id={"head": xt * 4 + zt}, device_id_type=MESH,
        )

    def gather(t2, idx):
        xo = 1 - xh
        return (
            lambda: part(t2, h, None, 0, xh, zp),
            lambda: part(t2, h, None, 1, xh, zm),
            lambda: part(t2, xh * 4 + zm, None, 2, xo, z),
            lambda: part(t2, xh * 4 + zp, None, 3, xo, z),
            lambda: part(t2, xh * 4 + zm, 0, 4, xh, zp),
            lambda: part(t2, xh * 4 + zp, 1, 5, xh, zm),
            lambda: part(t2, xo * 4 + zm, 0, 6, xh, zp),
            lambda: part(t2, xo * 4 + zm, 0, 7, xh, zm),
            lambda: part(t2, xo * 4 + zp, 1, 8, xh, zp),
            lambda: part(t2, xo * 4 + zp, 1, 9, xh, zm),
        )[idx]()

    def stage1(t2):
        gather(t2, 0).start()
        gather(t2, 1).start()

    def stage2(t2):
        wait_bytes(g_ref.at[t2, 0, pl.ds(0, 128)], ag_recv.at[t2, 0])
        for idx in range(2, 6):
            gather(t2, idx).start()

    def stage3(t2):
        wait_bytes(g_ref.at[t2, 0, pl.ds(0, 128)], ag_recv.at[t2, 1])
        for idx in range(6, 10):
            gather(t2, idx).start()

    order = (4, 2, 6, 1, 7, 3, 5)

    def halo(i, hh, which):
        ref = (k_ref, v_ref)[i]
        return pltpu.make_async_remote_copy(
            src_ref=ref.at[hh, 2 if which == 0 else 1], dst_ref=ref.at[hh, 0 if which == 0 else 3],
            send_sem=halo_ssem, recv_sem=halo_rsem.at[hh],
            device_id={"frame": right if which == 0 else left}, device_id_type=MESH,
        )

    def s1(t):
        return pltpu.make_async_remote_copy(
            src_ref=s1_send.at[t], dst_ref=s1_recv.at[t], send_sem=s1_ssem, recv_sem=s1_rsem.at[t],
            device_id={"frame": pair}, device_id_type=MESH,
        )

    far_cols = (pl.ds(384, 256), pl.ds(0, 384))
    near_cols = ((pl.ds(0, 384), pl.ds(384, 256)), (pl.ds(384, 256), pl.ds(0, 384)))

    def far(i):
        return pltpu.make_async_remote_copy(
            src_ref=far_send.at[:, far_cols[i]], dst_ref=far_recv.at[:, far_cols[i]],
            send_sem=far_ssem, recv_sem=far_rsem.at[i],
            device_id={"frame": up if i == 0 else down}, device_id_type=MESH,
        )

    def near(i, r):
        return pltpu.make_async_remote_copy(
            src_ref=near_send.at[i, :, near_cols[i][r]], dst_ref=near_recv.at[i, :, near_cols[i][r]],
            send_sem=near_ssem, recv_sem=near_rsem,
            device_id={"frame": up if i == 0 else down}, device_id_type=MESH,
        )

    def one_chunk(t2):
        wait_bytes(g_ref.at[t2, 0, pl.ds(0, 192)], ag_part.at[t2])
        gated = [
            (g_ref[t2, lf].astype(jnp.float32) * gain_ref[t2, pl.ds(lf, 1), :]).astype(jnp.bfloat16) for lf in range(2)
        ]
        rhs = jnp.concatenate(gated, axis=0)
        dacc[...] += dot(rhs, w_ref[t2], NT)
        return dot(ot_ref[...], rhs, NN) * (1.0 / tokens_all)

    def send_near(i, r):
        cols = near_cols[i][r]
        held = ((pl.ds(0, 384), pl.ds(0, 256)), (pl.ds(384, 256), pl.ds(256, 384)))[i][r]
        total = gsum[1 + r, :, held]
        if r == 1:
            far(i).wait_recv()
            total = total + far_recv[:, cols].astype(jnp.float32)
        near_send[i, :, cols] = total.astype(jnp.bfloat16)
        near(i, r).start()

    def send(names):
        for i, n in names:
            for p in order:
                exchange(i, n, p).start()

    for t2 in range(2):
        ((start, _, width),) = pieces(t2)
        for idx, to in ((0, zp), (1, zm)):
            pltpu.make_async_remote_copy(
                src_ref=c_hbm.at[:, :, pl.ds(pl.multiple_of(start, 128), width)], dst_ref=g_ref.at[t2, :, my_rows],
                send_sem=ag_send, recv_sem=ag_recv.at[t2, 0],
                device_id={"head": xh * 4 + to}, device_id_type=MESH,
            ).start()
    for p in order[:3]:
        o_exchange(p).start()
    o_copy.start()
    gate_copy.start()
    for copy in w_copies:
        copy.start()

    @pl.loop(0, heads)
    def _(hh):
        for i in range(3):
            own_copy(i, hh).start()

    stage2(0)
    pltpu.make_async_copy(g_ref.at[:, :, my_rows, :], g_ref.at[:, :, my_rows, :], c_sem).wait()
    stage2(1)
    for p in order[3:]:
        o_exchange(p).start()
    stage1(2)
    stage1(3)
    gate_copy.wait()
    for t2 in range(8):
        for start, at, width in pieces(t2):
            for lf in range(2):
                gain_ref[t2, pl.ds(lf, 1), pl.ds(at, width)] = gate_ref[
                    pl.ds(levels[lf], 1), pl.ds(pl.multiple_of(start, 128), width)
                ]

    def take(n):
        wait_bytes(k_ref.at[n, :, pl.ds(0, 224), :], ex_recv.at[n, 0])
        for i in range(2):
            halo(i, n, 0).start()
            halo(i, n, 1).start()

    def later(tt, u):
        @pl.when(tt < 3)
        def _():
            stage2(u + 2)

        @pl.when(tt < 2)
        def _():
            stage1(u + 4)

    @pl.loop(0, 5)
    def _(tt):
        t = tt - 1

        @pl.when(tt < 4)
        def _():
            stage3(2 * tt)

        later(tt, 2 * tt)

        @pl.when(tt >= 1)
        def _():
            gsum[t] = one_chunk(2 * t + 1)
            s1(t).wait_recv()
            gsum[t] += s1_recv[t].astype(jnp.float32)

        @pl.when(t == 0)
        def _():
            for i in range(2):
                far_send[:, far_cols[i]] = gsum[0, :, far_cols[i]].astype(jnp.bfloat16)
                far(i).start()

        @pl.when(t == 1)
        def _():
            send_near(0, 0)
            send_near(1, 0)

        @pl.when(t == 2)
        def _():
            send_near(0, 1)
            send_near(1, 1)

        @pl.when(tt < 4)
        def _():
            stage3(2 * tt + 1)

        later(tt, 2 * tt + 1)

        @pl.when(tt == 3)
        def _():
            send(((0, 0), (1, 0), (2, 0), (0, 1), (1, 1)))

        @pl.when(tt == 0)
        def _():
            o_copy.wait()
            wait_bytes(o_ref.at[:, pl.ds(0, 224), :], exo_recv)
            wait_bytes(o_ref.at[:, pl.ds(0, 224), :], exo_send)
            for lf in range(2):
                ot_ref[:, pl.ds(lf * TOKF, TOKF)] = o_ref[lf].astype(jnp.float32).T.astype(jnp.bfloat16)
            wait_bytes(w_ref, w_sem)
            wait_bytes(k_ref.at[0, :, pl.ds(0, 240), :], own_sem)
            dacc[...] = jnp.zeros_like(dacc)

        @pl.when(tt < 4)
        def _():
            s1_send[tt] = one_chunk(2 * tt).astype(jnp.bfloat16)
            s1(tt).start()

    send(((0, 2), (1, 2), (2, 1), (0, 3), (1, 3), (0, 4), (1, 4), (2, 2), (2, 3), (2, 4)))
    take(0)

    x_copy = pltpu.make_async_remote_copy(
        src_ref=x_send, dst_ref=x_recv, send_sem=x_ssem, recv_sem=x_rsem,
        device_id={"fsdp": 1 - s}, device_id_type=MESH,
    )

    def own_block():
        wait_bytes(near_recv, near_rsem)
        total = gsum[3] + near_recv[0].astype(jnp.float32) + near_recv[1].astype(jnp.float32)
        gsum[0] = total.T
        x_send[...] = gsum[0, pl.ds(pl.multiple_of(320 * (1 - s), 64), 320), :].astype(jnp.bfloat16)
        x_copy.start()

    def halo_grad(i, hh):
        return pltpu.make_async_remote_copy(
            src_ref=h_send.at[i, hh], dst_ref=h_recv.at[i, hh], send_sem=hg_ssem, recv_sem=hg_rsem.at[hh],
            device_id={"frame": left if i == 0 else right}, device_id_type=MESH,
        )

    def bias_of(fr, column, offset):
        target = fr + offset
        inside = (target >= 0) & (target < 2 * nf)
        chosen = flags[column, fr] == 1
        first = jnp.where(inside, 0.0, NEG).astype(jnp.float32)
        second = jnp.where(inside & chosen, 0.0, NEG).astype(jnp.float32)
        return first, second

    def attend(hh):
        hs = pl.ds(pl.multiple_of(hh * HD, 128), HD)
        for lf in range(2):
            q = q_ref[hh, lf]
            parts = []
            for w in range(3):
                sc = dot(k_ref[hh, lf + w], q, NT) * (inv_root * LOG2E)
                if w == 1:
                    parts.append(sc)
                else:
                    first, second = bias_of(2 * f + lf, 0 if w == 0 else 1, w - 1)
                    parts.append(jnp.concatenate([sc[:128] + first, sc[128:] + second], axis=0))
            m = functools.reduce(jnp.maximum, [jnp.max(x, axis=0, keepdims=True) for x in parts])
            parts = [jnp.exp2(x - m) for x in parts]
            total = functools.reduce(jnp.add, [jnp.sum(x, axis=0, keepdims=True) for x in parts])
            inv = 1.0 / total
            d_out = dacc[pl.ds(lf * TOKF, TOKF), hs].astype(jnp.bfloat16)
            delta = jnp.sum(
                (d_out.astype(jnp.float32) * o_ref[lf, :, hs].astype(jnp.float32)).T, axis=0, keepdims=True
            )
            dq_t = jnp.zeros((HD, TOKF), jnp.float32)
            for w in (0, 1, 2) if lf == 0 else (2, 1, 0):
                pr = parts[w] * inv
                dp = dot(v_ref[hh, lf + w], d_out, NT)
                ds = (pr * (dp - delta)).astype(jnp.bfloat16)
                gv = dot(pr.astype(jnp.bfloat16), d_out, NN)
                gk = dot(ds, q, NN) * inv_root
                slot = lf + w
                if slot in (0, 3):
                    h_send[slot // 3, hh, 0] = gk.astype(jnp.bfloat16)
                    h_send[slot // 3, hh, 1] = gv.astype(jnp.bfloat16)
                    halo_grad(slot // 3, hh).start()
                elif lf == 0:
                    own_k[hh, slot - 1] = gk
                    own_v[hh, slot - 1] = gv
                else:
                    own_k[hh, slot - 1] += gk
                    own_v[hh, slot - 1] += gv
                kt = k_ref[hh, lf + w].astype(jnp.float32).T.astype(jnp.bfloat16)
                dq_t = dq_t + dot(kt, ds, NN)
            dq_ref[lf, :, hs] = (dq_t.T * inv_root).astype(jnp.bfloat16)

    def finish(hh):
        hs = pl.ds(pl.multiple_of(hh * HD, 128), HD)
        wait_bytes(h_recv.at[:, hh], hg_rsem.at[hh])
        dk_ref[0, :, hs] = (own_k[hh, 0] + h_recv[1, hh, 0].astype(jnp.float32)).astype(jnp.bfloat16)
        dk_ref[1, :, hs] = (own_k[hh, 1] + h_recv[0, hh, 0].astype(jnp.float32)).astype(jnp.bfloat16)
        dv_ref[0, :, hs] = (own_v[hh, 0] + h_recv[1, hh, 1].astype(jnp.float32)).astype(jnp.bfloat16)
        dv_ref[1, :, hs] = (own_v[hh, 1] + h_recv[0, hh, 1].astype(jnp.float32)).astype(jnp.bfloat16)

    wait_bytes(g_ref.at[:, :, pl.ds(0, 224), :], ag_send)
    wait_bytes(s1_send, s1_ssem)
    wait_bytes(far_send, far_ssem)
    take(1)

    @pl.loop(0, heads)
    def _(n):
        @pl.when((n >= 1) & (n <= 2))
        def _():
            take(n + 1)

        @pl.when(n == 1)
        def _():
            own_block()

        @pl.when(n == 2)
        def _():
            take(4)

        wait_bytes(q_ref.at[n, :, pl.ds(0, 224), :], ex_recv.at[n, 1])
        wait_bytes(k_ref.at[n], halo_rsem.at[n])
        attend(n)

        @pl.when(n >= 2)
        def _():
            finish(n - 2)

    finish(heads - 2)
    wait_bytes(g_ref.at[pl.ds(0, 3), :, pl.ds(0, 224), :], ex_send)
    wait_bytes(k_ref, halo_ssem)
    wait_bytes(near_send, near_ssem)
    x_copy.wait_send()
    x_copy.wait_recv()
    dw_ref[...] = gsum[0, pl.ds(pl.multiple_of(320 * s, 64), 320), :] + x_recv[...].astype(jnp.float32)
    finish(heads - 1)
    wait_bytes(h_send, hg_ssem)


def write_out(*refs):
    copies = [pltpu.make_async_copy(refs[i], refs[4 + i], refs[8].at[i]) for i in range(4)]
    for copy in copies:
        copy.start()
    for copy in copies:
        copy.wait()


def per_device(
    queries, key_rows, value_rows, saved_out, cotangent, out_weight, gate_table, levels, reach_flags
):
    frame_dev = queries.shape[1]
    tokens_all = lax.axis_size("fsdp") * frame_dev * lax.axis_size("frame") * TOKF
    bf, f32 = jnp.bfloat16, jnp.float32
    vm = pltpu.VMEM
    dma = pltpu.SemaphoreType.DMA
    hbm = pl.BlockSpec(memory_space=pl.ANY)
    smem = pl.BlockSpec(memory_space=pltpu.SMEM)
    out = vm((2, TOKF, 640), bf)
    held = pl.pallas_call(
        functools.partial(kernel, tokens_all),
        out_shape=(out, out, out, vm((320, 640), f32)),
        in_specs=[smem, smem] + [hbm] * 7,
        out_specs=(pl.BlockSpec(memory_space=vm),) * 4,
        scratch_shapes=[
            vm((8, 640, 640), bf),
            vm((8, 2, TOKF, 640), bf),
            vm((5, 2, TOKF, HD), bf),
            vm((2, TOKF, 640), bf),
            vm((5, 4, TOKF, HD), bf),
            vm((5, 4, TOKF, HD), bf),
            vm((LEVELS, 5120), f32),
            vm((8, 2, 640), f32),
            vm((640, 2 * TOKF), bf),
            vm((2 * TOKF, 640), f32),
            vm((4, 640, 640), bf),
            vm((4, 640, 640), bf),
            vm((4, 640, 640), f32),
            vm((640, 640), bf),
            vm((640, 640), bf),
            vm((2, 640, 640), bf),
            vm((2, 640, 640), bf),
            vm((320, 640), bf),
            vm((320, 640), bf),
            vm((5, 2, TOKF, HD), f32),
            vm((5, 2, TOKF, HD), f32),
            vm((2, 5, 2, TOKF, HD), bf),
            vm((2, 5, 2, TOKF, HD), bf),
            dma((3,)), dma(()), dma(()), dma(()),
            dma(()), dma(()),
            dma(()), dma((5, 2)),
            dma(()), dma((8, 2)), dma((8,)),
            dma(()), dma((5,)),
            dma(()), dma((4,)),
            dma(()), dma((2,)),
            dma(()), dma(()),
            dma(()), dma(()),
            dma(()), dma((5,)),
        ],
        compiler_params=pltpu.CompilerParams(
            collective_id=0, has_side_effects=True, vmem_limit_bytes=58 * 2**20
        ),
        name="window_backward",
    )(
        reach_flags.T, levels, queries[0], key_rows[0], value_rows[0], saved_out[0], cotangent[0], out_weight, gate_table
    )
    out = jax.ShapeDtypeStruct((2, TOKF, 640), bf)
    dq, dk, dv, dw = pl.pallas_call(
        write_out,
        out_shape=(out, out, out, jax.ShapeDtypeStruct((320, 640), f32)),
        in_specs=[pl.BlockSpec(memory_space=vm)] * 4,
        out_specs=(hbm,) * 4,
        scratch_shapes=[dma((4,))],
        compiler_params=pltpu.CompilerParams(vmem_limit_bytes=4 * 2**20),
        name="write_out",
    )(*held)
    return (dq[None], dk[None], dv[None], dw.T)


def solution(mesh):
    in_specs = (
        P("fsdp", "frame", "head", None),
        P("fsdp", "frame", "head", None),
        P("fsdp", "frame", "head", None),
        P("fsdp", "frame", "head", None),
        P("fsdp", "frame", "head", None),
        P("head", None),
        P(),
        P("frame"),
        P(),
    )
    out_specs = (
        P("fsdp", "frame", None, "head"),
        P("fsdp", "frame", None, "head"),
        P("fsdp", "frame", None, "head"),
        P("head", ("frame", "fsdp")),
    )
    return jax.shard_map(
        per_device, mesh=mesh, in_specs=in_specs, out_specs=out_specs, check_vma=False
    )
```

```python
import functools

import jax
import jax.numpy as jnp
from jax import lax
from jax.experimental import pallas as pl
from jax.experimental.pallas import tpu as pltpu
from jax.sharding import PartitionSpec as P

HD = 128
LEVELS = 64
TOKF = 256
NEG = -1e30
LOG2E = 1.4426950408889634
MESH = pl.DeviceIdType.MESH

NT = (((1,), (1,)), ((), ()))
NN = (((1,), (0,)), ((), ()))


def dot(a, b, dims):
    return lax.dot_general(a, b, dims, preferred_element_type=jnp.float32)


def kernel(
    tokens_all, flags, levels,
    q_hbm, k_hbm, v_hbm, o_hbm, c_hbm, w_hbm, gate_hbm,
    dq_ref, dk_ref, dv_ref, dw_ref,
    w_ref, g_ref, q_ref, o_ref, k_ref, v_ref, gate_ref, gain_ref, ot_ref, dacc,
    s1_send, s1_recv, gsum, far_send, far_recv, near_send, near_recv, x_send, x_recv,
    own_k, own_v, h_send, h_recv,
    loc_sem, w_sem, c_sem, own_sem, exo_send, exo_recv, ex_send, ex_recv, ag_send, ag_recv, ag_part, halo_ssem, halo_rsem,
    s1_ssem, s1_rsem, far_ssem, far_rsem, near_ssem, near_rsem, x_ssem, x_rsem, hg_ssem, hg_rsem,
):
    f, h, s = lax.axis_index("frame"), lax.axis_index("head"), lax.axis_index("fsdp")
    nf = 8
    nh = 8
    y, c = f // 2, f % 2
    xh, z = h // 4, h % 4
    zp, zm = (z + 1) % 4, (z + 3) % 4
    right, left = (f + 1) % nf, (f + 7) % nf
    up, down = (f + 2) % nf, (f + 6) % nf
    pair = 2 * y + 1 - c
    rows = 32
    wid = 640
    heads = 5
    inv_root = HD ** (-0.5)

    def col(j):
        return pl.ds(pl.multiple_of(j * wid, 128), wid)

    def rows_of(n):
        return pl.ds(pl.multiple_of(n * rows, 32), rows)

    my_rows = rows_of(h)

    def pieces(t2):
        core = 1 - c if t2 % 2 == 0 else c
        ahead, back = ((y + 1) % 4 * 2 + core) * wid, ((y + 3) % 4 * 2 + core) * wid
        return (
            ((((y + 2) % 4 * 2 + core) * wid, 0, wid),),
            ((ahead, 0, 384), (back + 384, 384, 256)),
            ((ahead + 384, 0, 256), (back, 256, 384)),
            (((y * 2 + core) * wid, 0, wid),),
        )[t2 // 2]

    def head_cols(d, hh):
        return pl.ds(pl.multiple_of(d * wid + hh * HD, 128), HD)

    c_copies = []
    for t2 in range(8):
        for k, (start, at, width) in enumerate(pieces(t2)):
            c_copies.append(
                pltpu.make_async_copy(
                    c_hbm.at[:, :, pl.ds(pl.multiple_of(start, 128), width)],
                    g_ref.at[t2, :, my_rows, pl.ds(at, width)],
                    c_sem,
                )
            )
    gate_copy = pltpu.make_async_copy(gate_hbm, gate_ref, loc_sem.at[1])
    o_copy = pltpu.make_async_copy(o_hbm.at[:, :, col(h)], o_ref.at[:, my_rows, :], loc_sem.at[2])
    w_copies = []
    for t2 in range(8):
        for k, (start, at, width) in enumerate(pieces(t2)):
            w_copies.append(
                pltpu.make_async_copy(
                    w_hbm.at[:, pl.ds(pl.multiple_of(start, 128), width)], w_ref.at[t2, :, pl.ds(at, width)], w_sem
                )
            )

    def own_copy(i, hh):
        src, dst = (
            (k_hbm, k_ref.at[hh, pl.ds(1, 2), my_rows, :]),
            (v_hbm, v_ref.at[hh, pl.ds(1, 2), my_rows, :]),
            (q_hbm, q_ref.at[hh, :, my_rows, :]),
        )[i]
        return pltpu.make_async_copy(src.at[:, :, head_cols(h, hh)], dst, own_sem)

    barrier = pltpu.get_barrier_semaphore()
    for p in range(1, nh):
        pl.semaphore_signal(barrier, inc=1, device_id={"head": (h + p) % nh}, device_id_type=MESH)
    for other in (right, left, up, down):
        pl.semaphore_signal(barrier, inc=1, device_id={"frame": other}, device_id_type=MESH)
    pl.semaphore_signal(barrier, inc=1, device_id={"fsdp": 1 - s}, device_id_type=MESH)
    for copy in c_copies:
        copy.start()
    pl.semaphore_wait(barrier, nh - 1 + 5)

    def wait_bytes(ref, sem):
        pltpu.make_async_copy(ref, ref, sem).wait()

    def o_exchange(p):
        d = (h + p) % nh
        return pltpu.make_async_remote_copy(
            src_ref=o_hbm.at[:, :, col(d)], dst_ref=o_ref.at[:, my_rows, :],
            send_sem=exo_send, recv_sem=exo_recv,
            device_id={"head": d}, device_id_type=MESH,
        )

    def exchange(i, hh, p):
        d = (h + p) % nh
        src, dst = (
            (k_hbm, k_ref.at[hh, pl.ds(1, 2), my_rows, :]),
            (v_hbm, v_ref.at[hh, pl.ds(1, 2), my_rows, :]),
            (q_hbm, q_ref.at[hh, :, my_rows, :]),
        )[i]
        return pltpu.make_async_remote_copy(
            src_ref=src.at[:, :, head_cols(d, hh)], dst_ref=dst,
            send_sem=ex_send, recv_sem=ex_recv.at[hh, i // 2],
            device_id={"head": d}, device_id_type=MESH,
        )

    def part(t2, n, half, idx, xt, zt):
        ref = g_ref.at[t2, :, rows_of(n)] if half is None else g_ref.at[t2, half, rows_of(n)]
        return pltpu.make_async_remote_copy(
            src_ref=ref, dst_ref=ref, send_sem=ag_send, recv_sem=ag_recv.at[t2, idx // 2] if idx < 4 else ag_part.at[t2],
            device_id={"head": xt * 4 + zt}, device_id_type=MESH,
        )

    def gather(t2, idx):
        xo = 1 - xh
        return (
            lambda: part(t2, h, None, 0, xh, zp),
            lambda: part(t2, h, None, 1, xh, zm),
            lambda: part(t2, xh * 4 + zm, None, 2, xo, z),
            lambda: part(t2, xh * 4 + zp, None, 3, xo, z),
            lambda: part(t2, xh * 4 + zm, 0, 4, xh, zp),
            lambda: part(t2, xh * 4 + zp, 1, 5, xh, zm),
            lambda: part(t2, xo * 4 + zm, 0, 6, xh, zp),
            lambda: part(t2, xo * 4 + zm, 0, 7, xh, zm),
            lambda: part(t2, xo * 4 + zp, 1, 8, xh, zp),
            lambda: part(t2, xo * 4 + zp, 1, 9, xh, zm),
        )[idx]()

    def stage1(t2):
        gather(t2, 0).start()
        gather(t2, 1).start()

    def stage2(t2):
        wait_bytes(g_ref.at[t2, 0, pl.ds(0, 128)], ag_recv.at[t2, 0])
        for idx in range(2, 6):
            gather(t2, idx).start()

    def stage3(t2):
        wait_bytes(g_ref.at[t2, 0, pl.ds(0, 128)], ag_recv.at[t2, 1])
        for idx in range(6, 10):
            gather(t2, idx).start()

    order = (4, 2, 6, 1, 7, 3, 5)

    def halo(i, hh, which):
        ref = (k_ref, v_ref)[i]
        return pltpu.make_async_remote_copy(
            src_ref=ref.at[hh, 2 if which == 0 else 1], dst_ref=ref.at[hh, 0 if which == 0 else 3],
            send_sem=halo_ssem, recv_sem=halo_rsem.at[hh],
            device_id={"frame": right if which == 0 else left}, device_id_type=MESH,
        )

    def s1(t):
        return pltpu.make_async_remote_copy(
            src_ref=s1_send.at[t], dst_ref=s1_recv.at[t], send_sem=s1_ssem, recv_sem=s1_rsem.at[t],
            device_id={"frame": pair}, device_id_type=MESH,
        )

    far_cols = (pl.ds(384, 256), pl.ds(0, 384))
    near_cols = ((pl.ds(0, 384), pl.ds(384, 256)), (pl.ds(384, 256), pl.ds(0, 384)))

    def far(i):
        return pltpu.make_async_remote_copy(
            src_ref=far_send.at[:, far_cols[i]], dst_ref=far_recv.at[:, far_cols[i]],
            send_sem=far_ssem, recv_sem=far_rsem.at[i],
            device_id={"frame": up if i == 0 else down}, device_id_type=MESH,
        )

    def near(i, r):
        return pltpu.make_async_remote_copy(
            src_ref=near_send.at[i, :, near_cols[i][r]], dst_ref=near_recv.at[i, :, near_cols[i][r]],
            send_sem=near_ssem, recv_sem=near_rsem,
            device_id={"frame": up if i == 0 else down}, device_id_type=MESH,
        )

    def one_chunk(t2):
        wait_bytes(g_ref.at[t2, 0, pl.ds(0, 192)], ag_part.at[t2])
        gated = [
            (g_ref[t2, lf].astype(jnp.float32) * gain_ref[t2, pl.ds(lf, 1), :]).astype(jnp.bfloat16) for lf in range(2)
        ]
        rhs = jnp.concatenate(gated, axis=0)
        dacc[...] += dot(rhs, w_ref[t2], NT)
        return dot(ot_ref[...], rhs, NN) * (1.0 / tokens_all)

    def send_near(i, r):
        cols = near_cols[i][r]
        held = ((pl.ds(0, 384), pl.ds(0, 256)), (pl.ds(384, 256), pl.ds(256, 384)))[i][r]
        total = gsum[1 + r, :, held]
        if r == 1:
            far(i).wait_recv()
            total = total + far_recv[:, cols].astype(jnp.float32)
        near_send[i, :, cols] = total.astype(jnp.bfloat16)
        near(i, r).start()

    def send(names):
        for i, n in names:
            for p in order:
                exchange(i, n, p).start()

    for t2 in range(2):
        ((start, _, width),) = pieces(t2)
        for idx, to in ((0, zp), (1, zm)):
            pltpu.make_async_remote_copy(
                src_ref=c_hbm.at[:, :, pl.ds(pl.multiple_of(start, 128), width)], dst_ref=g_ref.at[t2, :, my_rows],
                send_sem=ag_send, recv_sem=ag_recv.at[t2, 0],
                device_id={"head": xh * 4 + to}, device_id_type=MESH,
            ).start()
    for p in order[:3]:
        o_exchange(p).start()
    o_copy.start()
    gate_copy.start()
    for copy in w_copies:
        copy.start()

    @pl.loop(0, heads)
    def _(hh):
        for i in range(3):
            own_copy(i, hh).start()

    stage2(0)
    pltpu.make_async_copy(g_ref.at[:, :, my_rows, :], g_ref.at[:, :, my_rows, :], c_sem).wait()
    stage2(1)
    for p in order[3:]:
        o_exchange(p).start()
    stage1(2)
    stage1(3)
    gate_copy.wait()
    for t2 in range(8):
        for start, at, width in pieces(t2):
            for lf in range(2):
                gain_ref[t2, pl.ds(lf, 1), pl.ds(at, width)] = gate_ref[
                    pl.ds(levels[lf], 1), pl.ds(pl.multiple_of(start, 128), width)
                ]

    def take(n):
        wait_bytes(k_ref.at[n, :, pl.ds(0, 224), :], ex_recv.at[n, 0])
        for i in range(2):
            halo(i, n, 0).start()
            halo(i, n, 1).start()

    def later(tt, u):
        @pl.when(tt < 3)
        def _():
            stage2(u + 2)

        @pl.when(tt < 2)
        def _():
            stage1(u + 4)

    @pl.loop(0, 5)
    def _(tt):
        t = tt - 1

        @pl.when(tt < 4)
        def _():
            stage3(2 * tt)

        later(tt, 2 * tt)

        @pl.when(tt >= 1)
        def _():
            gsum[t] = one_chunk(2 * t + 1)
            s1(t).wait_recv()
            gsum[t] += s1_recv[t].astype(jnp.float32)

        @pl.when(t == 0)
        def _():
            for i in range(2):
                far_send[:, far_cols[i]] = gsum[0, :, far_cols[i]].astype(jnp.bfloat16)
                far(i).start()

        @pl.when(t == 1)
        def _():
            send_near(0, 0)
            send_near(1, 0)

        @pl.when(t == 2)
        def _():
            send_near(0, 1)
            send_near(1, 1)

        @pl.when(tt < 4)
        def _():
            stage3(2 * tt + 1)

        later(tt, 2 * tt + 1)

        @pl.when(tt == 3)
        def _():
            send(((0, 0), (1, 0), (2, 0), (0, 1), (1, 1)))

        @pl.when(tt == 0)
        def _():
            o_copy.wait()
            wait_bytes(o_ref.at[:, pl.ds(0, 224), :], exo_recv)
            wait_bytes(o_ref.at[:, pl.ds(0, 224), :], exo_send)
            for lf in range(2):
                ot_ref[:, pl.ds(lf * TOKF, TOKF)] = o_ref[lf].astype(jnp.float32).T.astype(jnp.bfloat16)
            wait_bytes(w_ref, w_sem)
            wait_bytes(k_ref.at[0, :, pl.ds(0, 240), :], own_sem)
            dacc[...] = jnp.zeros_like(dacc)

        @pl.when(tt < 4)
        def _():
            s1_send[tt] = one_chunk(2 * tt).astype(jnp.bfloat16)
            s1(tt).start()

    send(((0, 2), (1, 2), (2, 1), (0, 3), (1, 3), (0, 4), (1, 4), (2, 2), (2, 3), (2, 4)))
    take(0)

    x_copy = pltpu.make_async_remote_copy(
        src_ref=x_send, dst_ref=x_recv, send_sem=x_ssem, recv_sem=x_rsem,
        device_id={"fsdp": 1 - s}, device_id_type=MESH,
    )

    def own_block():
        wait_bytes(near_recv, near_rsem)
        total = gsum[3] + near_recv[0].astype(jnp.float32) + near_recv[1].astype(jnp.float32)
        gsum[0] = total.T
        x_send[...] = gsum[0, pl.ds(pl.multiple_of(320 * (1 - s), 64), 320), :].astype(jnp.bfloat16)
        x_copy.start()

    def halo_grad(i, hh):
        return pltpu.make_async_remote_copy(
            src_ref=h_send.at[i, hh], dst_ref=h_recv.at[i, hh], send_sem=hg_ssem, recv_sem=hg_rsem.at[hh],
            device_id={"frame": left if i == 0 else right}, device_id_type=MESH,
        )

    def bias_of(fr, column, offset):
        target = fr + offset
        inside = (target >= 0) & (target < 2 * nf)
        chosen = flags[column, fr] == 1
        first = jnp.where(inside, 0.0, NEG).astype(jnp.float32)
        second = jnp.where(inside & chosen, 0.0, NEG).astype(jnp.float32)
        return first, second

    def attend(hh):
        hs = pl.ds(pl.multiple_of(hh * HD, 128), HD)
        for lf in range(2):
            q = q_ref[hh, lf]
            parts = []
            for w in range(3):
                sc = dot(k_ref[hh, lf + w], q, NT) * (inv_root * LOG2E)
                if w == 1:
                    parts.append(sc)
                else:
                    first, second = bias_of(2 * f + lf, 0 if w == 0 else 1, w - 1)
                    parts.append(jnp.concatenate([sc[:128] + first, sc[128:] + second], axis=0))
            m = functools.reduce(jnp.maximum, [jnp.max(x, axis=0, keepdims=True) for x in parts])
            parts = [jnp.exp2(x - m) for x in parts]
            total = functools.reduce(jnp.add, [jnp.sum(x, axis=0, keepdims=True) for x in parts])
            inv = 1.0 / total
            d_out = dacc[pl.ds(lf * TOKF, TOKF), hs].astype(jnp.bfloat16)
            delta = jnp.sum(
                (d_out.astype(jnp.float32) * o_ref[lf, :, hs].astype(jnp.float32)).T, axis=0, keepdims=True
            )
            dq_t = jnp.zeros((HD, TOKF), jnp.float32)
            for w in (0, 1, 2) if lf == 0 else (2, 1, 0):
                pr = parts[w] * inv
                dp = dot(v_ref[hh, lf + w], d_out, NT)
                ds = (pr * (dp - delta)).astype(jnp.bfloat16)
                gv = dot(pr.astype(jnp.bfloat16), d_out, NN)
                gk = dot(ds, q, NN) * inv_root
                slot = lf + w
                if slot in (0, 3):
                    h_send[slot // 3, hh, 0] = gk.astype(jnp.bfloat16)
                    h_send[slot // 3, hh, 1] = gv.astype(jnp.bfloat16)
                    halo_grad(slot // 3, hh).start()
                elif lf == 0:
                    own_k[hh, slot - 1] = gk
                    own_v[hh, slot - 1] = gv
                else:
                    own_k[hh, slot - 1] += gk
                    own_v[hh, slot - 1] += gv
                kt = k_ref[hh, lf + w].astype(jnp.float32).T.astype(jnp.bfloat16)
                dq_t = dq_t + dot(kt, ds, NN)
            dq_ref[lf, :, hs] = (dq_t.T * inv_root).astype(jnp.bfloat16)

    def finish(hh):
        hs = pl.ds(pl.multiple_of(hh * HD, 128), HD)
        wait_bytes(h_recv.at[:, hh], hg_rsem.at[hh])
        dk_ref[0, :, hs] = (own_k[hh, 0] + h_recv[1, hh, 0].astype(jnp.float32)).astype(jnp.bfloat16)
        dk_ref[1, :, hs] = (own_k[hh, 1] + h_recv[0, hh, 0].astype(jnp.float32)).astype(jnp.bfloat16)
        dv_ref[0, :, hs] = (own_v[hh, 0] + h_recv[1, hh, 1].astype(jnp.float32)).astype(jnp.bfloat16)
        dv_ref[1, :, hs] = (own_v[hh, 1] + h_recv[0, hh, 1].astype(jnp.float32)).astype(jnp.bfloat16)

    wait_bytes(g_ref.at[:, :, pl.ds(0, 224), :], ag_send)
    wait_bytes(s1_send, s1_ssem)
    wait_bytes(far_send, far_ssem)
    take(1)

    @pl.loop(0, heads)
    def _(n):
        @pl.when((n >= 1) & (n <= 2))
        def _():
            take(n + 1)

        @pl.when(n == 1)
        def _():
            own_block()

        @pl.when(n == 2)
        def _():
            take(4)

        wait_bytes(q_ref.at[n, :, pl.ds(0, 224), :], ex_recv.at[n, 1])
        wait_bytes(k_ref.at[n], halo_rsem.at[n])
        attend(n)

        @pl.when(n >= 2)
        def _():
            finish(n - 2)

    finish(heads - 2)
    wait_bytes(g_ref.at[pl.ds(0, 3), :, pl.ds(0, 224), :], ex_send)
    wait_bytes(k_ref, halo_ssem)
    wait_bytes(near_send, near_ssem)
    x_copy.wait_send()
    x_copy.wait_recv()
    dw_ref[...] = gsum[0, pl.ds(pl.multiple_of(320 * s, 64), 320), :] + x_recv[...].astype(jnp.float32)
    finish(heads - 1)
    wait_bytes(h_send, hg_ssem)


def write_out(*refs):
    copies = []
    for i in range(4):
        for half in range(2):
            at = half if i < 3 else pl.ds(160 * half, 160)
            copies.append(pltpu.make_async_copy(refs[i].at[at], refs[4 + i].at[at], refs[8].at[i, half]))
    for copy in copies:
        copy.start()
    for copy in copies:
        copy.wait()


def per_device(
    queries, key_rows, value_rows, saved_out, cotangent, out_weight, gate_table, levels, reach_flags
):
    frame_dev = queries.shape[1]
    tokens_all = lax.axis_size("fsdp") * frame_dev * lax.axis_size("frame") * TOKF
    bf, f32 = jnp.bfloat16, jnp.float32
    vm = pltpu.VMEM
    dma = pltpu.SemaphoreType.DMA
    hbm = pl.BlockSpec(memory_space=pl.ANY)
    smem = pl.BlockSpec(memory_space=pltpu.SMEM)
    out = vm((2, TOKF, 640), bf)
    held = pl.pallas_call(
        functools.partial(kernel, tokens_all),
        out_shape=(out, out, out, vm((320, 640), f32)),
        in_specs=[smem, smem] + [hbm] * 7,
        out_specs=(pl.BlockSpec(memory_space=vm),) * 4,
        scratch_shapes=[
            vm((8, 640, 640), bf),
            vm((8, 2, TOKF, 640), bf),
            vm((5, 2, TOKF, HD), bf),
            vm((2, TOKF, 640), bf),
            vm((5, 4, TOKF, HD), bf),
            vm((5, 4, TOKF, HD), bf),
            vm((LEVELS, 5120), f32),
            vm((8, 2, 640), f32),
            vm((640, 2 * TOKF), bf),
            vm((2 * TOKF, 640), f32),
            vm((4, 640, 640), bf),
            vm((4, 640, 640), bf),
            vm((4, 640, 640), f32),
            vm((640, 640), bf),
            vm((640, 640), bf),
            vm((2, 640, 640), bf),
            vm((2, 640, 640), bf),
            vm((320, 640), bf),
            vm((320, 640), bf),
            vm((5, 2, TOKF, HD), f32),
            vm((5, 2, TOKF, HD), f32),
            vm((2, 5, 2, TOKF, HD), bf),
            vm((2, 5, 2, TOKF, HD), bf),
            dma((3,)), dma(()), dma(()), dma(()),
            dma(()), dma(()),
            dma(()), dma((5, 2)),
            dma(()), dma((8, 2)), dma((8,)),
            dma(()), dma((5,)),
            dma(()), dma((4,)),
            dma(()), dma((2,)),
            dma(()), dma(()),
            dma(()), dma(()),
            dma(()), dma((5,)),
        ],
        compiler_params=pltpu.CompilerParams(
            collective_id=0, has_side_effects=True, vmem_limit_bytes=58 * 2**20
        ),
        name="window_backward",
    )(
        reach_flags.T, levels, queries[0], key_rows[0], value_rows[0], saved_out[0], cotangent[0], out_weight, gate_table
    )
    out = jax.ShapeDtypeStruct((2, TOKF, 640), bf)
    dq, dk, dv, dw = pl.pallas_call(
        write_out,
        out_shape=(out, out, out, jax.ShapeDtypeStruct((320, 640), f32)),
        in_specs=[pl.BlockSpec(memory_space=vm)] * 4,
        out_specs=(hbm,) * 4,
        scratch_shapes=[dma((4, 2))],
        compiler_params=pltpu.CompilerParams(vmem_limit_bytes=4 * 2**20),
        name="write_out",
    )(*held)
    return (dq[None], dk[None], dv[None], dw.T)


def solution(mesh):
    in_specs = (
        P("fsdp", "frame", "head", None),
        P("fsdp", "frame", "head", None),
        P("fsdp", "frame", "head", None),
        P("fsdp", "frame", "head", None),
        P("fsdp", "frame", "head", None),
        P("head", None),
        P(),
        P("frame"),
        P(),
    )
    out_specs = (
        P("fsdp", "frame", None, "head"),
        P("fsdp", "frame", None, "head"),
        P("fsdp", "frame", None, "head"),
        P("head", ("frame", "fsdp")),
    )
    return jax.shard_map(
        per_device, mesh=mesh, in_specs=in_specs, out_specs=out_specs, check_vma=False
    )
```
